768 devices in a mesh: gx: 12 (over z), gy: 64 (over y, x, core).
Axes of the slice: x: 4, y: 8, z: 12, core: 2. Of those that a mesh axis runs over, the one named last changes fastest.
Arguments:
- temps: float32 [2, 384, 768, 128], P(None, 'gx', 'gy'), may hold values from 0.5 to 2
- right_side: float32 [2, 384, 768, 128], P(None, 'gx', 'gy'), may hold values from -5 to 5
- exchange: float32 [384, 768, 128], P('gx', 'gy'), may hold values from 0.1 to 1
- coupling: float32 [384, 768, 128], P('gx', 'gy'), may hold values from 0.05 to 0.5
Outputs:
- fields: float32 [2, 384, 768, 128], P(None, 'gx', 'gy')
The draws below stay inside these ranges and needn't reach their ends.
All inputs are finite; a program needn't handle non-finite values.
Results may differ from the reference program's by a relative error of at most 0.000027.
Values sent between devices are 32-bit elements; how exact they have to be, the bound alone decides.
A program may use at most 64 MiB of HBM per device.

```python
import math
import jax
import jax.numpy as jnp
from jax import lax

NZ = 128
SWEEPS = 2
NX = 384
NY = 768


def draw_right_side(key, part):
    shape = (2, NX, NY, NZ)
    return jnp.clip(jax.random.normal(key, shape, jnp.float32), -5.0, 5.0)


def shard_levels(key, shape, shards, least, top_value):
    gain, own = 1.0, jax.random.fold_in(key, 6)
    for axis_at, parts in shards:
        draws = jnp.exp(jax.random.uniform(jax.random.fold_in(own, axis_at), (parts,), jnp.float32, least / len(shards), top_value / len(shards)))
        gain = gain * jnp.repeat(draws, shape[axis_at] // parts).reshape([-1 if axis == axis_at else 1 for axis in range(len(shape))])
    return gain


def setup_inputs(seed: int = 0) -> dict:
    key_list = jax.random.split(jax.random.key(seed), 5)
    return {
        "temps": jnp.clip(0.5 + 1.5 * jax.random.uniform(key_list[0], (2, NX, NY, NZ), jnp.float32) ** shard_levels(key_list[0], (2, NX, NY, NZ), ((1, 12), (2, 64)), -0.2, 0.2), 0.5, 2.0),
        "right_side": draw_right_side(jax.random.fold_in(key_list[4], 71), 0),
        "exchange": jnp.clip(jnp.exp(math.log(1.0) - 2.3025851 * jax.random.uniform(key_list[2], (NX, NY, NZ), jnp.float32) ** shard_levels(key_list[2], (NX, NY, NZ), ((0, 12), (1, 64)), -0.2, 0.2)), 0.1, 1.0),
        "coupling": jnp.clip(jnp.exp(math.log(0.5) - 2.3025851 * jax.random.uniform(key_list[3], (NX, NY, NZ), jnp.float32) ** shard_levels(key_list[3], (NX, NY, NZ), ((0, 12), (1, 64)), -0.2, 0.2)), 0.05, 0.5),
    }


solid_cap = 0.5
gas_cap = 0.02
flow_rate = 40.0
gas_conduct = 0.05
axis_weights = (1.0, 1.0, 1.0, 1.0, 0.25, 0.25)
relaxation = 0.8
lump_factor = 0.25


def neighbours(padded):
    center = padded[1:-1, 1:-1]
    z_padded = jnp.pad(center, ((0, 0), (0, 0), (1, 1)))
    return center, (padded[2:, 1:-1], padded[:-2, 1:-1], padded[1:-1, 2:], padded[1:-1, :-2], z_padded[:, :, 2:], z_padded[:, :, :-2])


def face_weights(cond_padded):
    conductivity, beside_all = neighbours(cond_padded)
    return tuple(weight * 0.5 * (conductivity + other) for weight, other in zip(axis_weights, beside_all))


def apply_operator(fields_padded, face_list, coupling):
    solid, solid_around = neighbours(fields_padded[0])
    gas, gas_around = neighbours(fields_padded[1])
    exchange_term = coupling * (solid - gas)
    solid_out = solid_cap * solid + exchange_term
    gas_out = gas_cap * gas - exchange_term + flow_rate * (gas - gas_around[3])
    for face, weight, other_solid, other_gas in zip(face_list, axis_weights, solid_around, gas_around):
        solid_out = solid_out + face * (solid - other_solid)
        gas_out = gas_out + gas_conduct * weight * (gas - other_gas)
    return jnp.stack([solid_out, gas_out])


def relax_step(fields, residual, solid_diag, coupling):
    gas_diag = gas_cap + coupling + flow_rate + gas_conduct * 2.0 * 2.25
    determinant = solid_diag * gas_diag - coupling * coupling
    delta_solid = (gas_diag * residual[0] + coupling * residual[1]) / determinant
    delta_gas = (coupling * residual[0] + solid_diag * residual[1]) / determinant
    return fields + relaxation * jnp.stack([delta_solid, delta_gas])


def coarse_sum(array):
    shape = array.shape
    lead = shape[:-3]
    return array.reshape(lead + (shape[-3] // 2, 2, shape[-2] // 2, 2, shape[-1])).sum(axis=(-4, -2))


def spread(coarse):
    shape = coarse.shape
    wide = jnp.broadcast_to(coarse[:, :, None, :, None, :], (shape[0], shape[1], 2, shape[2], 2, shape[3]))
    return wide.reshape((shape[0], shape[1] * 2, shape[2] * 2, shape[3]))


def line_combine(earlier, later):
    return (later[0] * earlier[0], later[0] * earlier[1] + later[1])


def reference(temps, right_side, exchange, coupling):
    conductivity = 1.0 + 4.0 * exchange * temps[0] ** 3
    face_list = face_weights(jnp.pad(conductivity, ((1, 1), (1, 1), (0, 0))))
    solid_diag = solid_cap + coupling + sum(face_list)

    def residual_of(fields):
        padded = jnp.pad(fields, ((0, 0), (1, 1), (1, 1), (0, 0)))
        return right_side - apply_operator(padded, face_list, coupling)

    fields = temps
    for sweep_index in range(SWEEPS):
        fields = relax_step(fields, residual_of(fields), solid_diag, coupling)
    coarse_res = coarse_sum(residual_of(fields))
    coupling_sum = coarse_sum(coupling)
    solid_coarse = 4.0 * solid_cap + coupling_sum + lump_factor * coarse_sum(conductivity)
    gas_coarse = 4.0 * gas_cap + coupling_sum + 2.0 * flow_rate
    denominator = gas_coarse - coupling_sum * coupling_sum / solid_coarse
    slope = 2.0 * flow_rate / denominator
    offset = (coarse_res[1] + coupling_sum * coarse_res[0] / solid_coarse) / denominator
    slope_cum, gas_error = lax.associative_scan(line_combine, (slope, offset), axis=1)
    solid_error = (coarse_res[0] + coupling_sum * gas_error) / solid_coarse
    fields = fields + spread(jnp.stack([solid_error, gas_error]))
    for sweep_index in range(SWEEPS):
        fields = relax_step(fields, residual_of(fields), solid_diag, coupling)
    return fields
```

```python
import functools

import jax
import jax.numpy as jnp
from jax import lax
from jax.experimental import pallas as pl
from jax.experimental.pallas import tpu as pltpu
from jax.sharding import PartitionSpec as P

MESH = pl.DeviceIdType.MESH
PITCH = 16
CHUNK = 64

solid_cap = 0.5
gas_cap = 0.02
flow_rate = 40.0
gas_conduct = 0.05
relaxation = 0.8
lump_factor = 0.25
STAGES = 5


def kernel(dims, temps, right, exch, coup, out, *scratch):
    nx, ny, nz, n_gx, n_gy, group = dims
    rows = nx * PITCH
    cx, cy = nx // 2, ny // 2
    n_group = n_gy // group
    (t_in, b_in, e_in, c_in, o_v, f0, f1, f2, f3, f4, b_f, c_f, fx, fy, fz, diag, pp, qq, rr, res,
     ys, yr, slopes, csum, isol, iden, cres, offs, s_blk, o_blk, s_rec, o_rec, s_row, o_row, s_rrec, o_rrec, s_pre,
     in_sem, h_send, h_recv, g_send, g_recv) = scratch
    ix, iy = lax.axis_index("gx"), lax.axis_index("gy")
    place, row = lax.rem(iy, group), lax.div(iy, group)

    loads = [
        pltpu.make_async_copy(src, dst, in_sem.at[i])
        for i, (src, dst) in enumerate(((temps, t_in), (exch, e_in), (coup, c_in), (right, b_in)))
    ]
    for load in loads:
        load.start()

    barrier = pltpu.get_barrier_semaphore()

    def greet(gx, gy):
        pl.semaphore_signal(barrier, inc=1, device_id=(gx, gy), device_id_type=MESH)

    for d in range(1, group):
        greet(ix, row * group + lax.rem(place + d, group))
    for d in range(1, n_group):
        greet(ix, lax.rem(row + d, n_group) * group + place)
    up_y, down_y, up_x, down_x = iy < n_gy - 1, iy > 0, ix < n_gx - 1, ix > 0
    pl.when(up_y)(lambda: greet(ix, iy + 1))
    pl.when(down_y)(lambda: greet(ix, iy - 1))
    pl.when(up_x)(lambda: greet(ix + 1, iy))
    pl.when(down_x)(lambda: greet(ix - 1, iy))

    fields = (f0, f1, f2, f3, f4)
    slab_zero = jnp.zeros((PITCH, nz), jnp.float32)
    plane_zero = jnp.zeros((nx, nz), jnp.float32)

    def clear_slabs(at):
        for f in fields:
            for n in range(f.shape[0]):
                f[n, at:at + PITCH, :] = slab_zero

    def clear_planes(side):
        for st in range(STAGES):
            for n in range(3 if st == 0 else 2):
                yr[st, side, n] = plane_zero

    pl.when(jnp.logical_not(down_x))(lambda: clear_slabs(0))
    pl.when(jnp.logical_not(up_x))(lambda: clear_slabs(rows + PITCH))
    pl.when(jnp.logical_not(down_y))(lambda: clear_planes(0))
    pl.when(jnp.logical_not(up_y))(lambda: clear_planes(1))
    for d in range(1, n_group):

        @pl.when(row < d)
        def _():
            s_rrec[d - 1] = jnp.ones((cx, nz), jnp.float32)
            o_rrec[d - 1] = jnp.zeros((cx, nz), jnp.float32)

    def halo_copies(st):
        f = fields[st]
        nf = f.shape[0]
        parts = (
            (up_y, down_y, ys.at[st, 1, :nf], yr.at[st, 0, :nf], (ix, iy + 1)),
            (down_y, up_y, ys.at[st, 0, :nf], yr.at[st, 1, :nf], (ix, iy - 1)),
            (up_x, down_x, f.at[:, rows:rows + PITCH], f.at[:, 0:PITCH], (ix + 1, iy)),
            (down_x, up_x, f.at[:, PITCH:2 * PITCH], f.at[:, rows + PITCH:rows + 2 * PITCH], (ix - 1, iy)),
        )
        return [
            (sends, receives, pltpu.make_async_remote_copy(
                src_ref=src, dst_ref=dst, send_sem=h_send.at[st, i], recv_sem=h_recv.at[st, i],
                device_id=to, device_id_type=MESH))
            for i, (sends, receives, src, dst, to) in enumerate(parts)
        ]

    def send_halo(st):
        f = fields[st]
        for n in range(f.shape[0]):
            ys[st, 0, n] = f[n, pl.ds(PITCH, nx, stride=PITCH), :]
            ys[st, 1, n] = f[n, pl.ds(PITCH + ny - 1, nx, stride=PITCH), :]
        for sends, _, copy in halo_copies(st):
            pl.when(sends)(copy.start)

    def take_halo(st):
        f = fields[st]
        for sends, receives, copy in halo_copies(st):
            pl.when(sends)(copy.wait_send)
            pl.when(receives)(copy.wait_recv)
        for n in range(f.shape[0]):
            f[n, pl.ds(PITCH - 1, nx, stride=PITCH), :] = yr[st, 0, n]
            f[n, pl.ds(PITCH + ny, nx, stride=PITCH), :] = yr[st, 1, n]

    def group_copies(kind, block, received):
        return [
            pltpu.make_async_remote_copy(
                src_ref=block, dst_ref=received.at[d - 1],
                send_sem=g_send.at[kind, d - 1], recv_sem=g_recv.at[kind, d - 1],
                device_id=(ix, row * group + lax.rem(place + d, group)), device_id_type=MESH)
            for d in range(1, group)
        ]

    def row_copies(kind, block, received):
        return [
            (row + d < n_group, row >= d, pltpu.make_async_remote_copy(
                src_ref=block, dst_ref=received.at[d - 1],
                send_sem=g_send.at[kind, d - 1], recv_sem=g_recv.at[kind, d - 1],
                device_id=(ix, (row + d) * group + place), device_id_type=MESH))
            for d in range(1, n_group)
        ]

    loads[0].wait()
    loads[1].wait()

    def spread_in(x, _):
        at = pl.multiple_of((x + 1) * PITCH, PITCH)
        s = t_in[0, x]
        f0[0, pl.ds(at, ny), :] = s
        f0[1, pl.ds(at, ny), :] = t_in[1, x]
        f0[2, pl.ds(at, ny), :] = 1.0 + 4.0 * e_in[x] * (s * s * s)
        return 0

    lax.fori_loop(0, nx, spread_in, 0, unroll=4)
    n_halo = sum(v.astype(jnp.int32) for v in (up_y, down_y, up_x, down_x))
    pl.semaphore_wait(barrier, (group - 1) + (n_group - 1) + n_halo)
    send_halo(0)

    loads[2].wait()
    loads[3].wait()

    def spread_more(x, _):
        at = pl.multiple_of(x * PITCH, PITCH)
        c_f[pl.ds(at, ny), :] = c_in[x]
        b_f[0, pl.ds(at, ny), :] = b_in[0, x]
        b_f[1, pl.ds(at, ny), :] = b_in[1, x]
        return 0

    lax.fori_loop(0, nx, spread_more, 0, unroll=4)

    def block_sum(load, j):
        total = None
        for a in (0, PITCH):
            for b in (0, 1):
                part = load(pl.ds(2 * j + a + b, cx, stride=2 * PITCH))
                total = part if total is None else total + part
        return total

    s_all = None
    for j in range(cy):
        cs = block_sum(lambda at: c_f[at, :], j)
        cond = block_sum(lambda at: f0[2, pl.ds(at.start + PITCH, at.size, stride=at.stride), :], j)
        inv_solid = 1.0 / (4.0 * solid_cap + cs + lump_factor * cond)
        inv_denom = 1.0 / (4.0 * gas_cap + cs + 2.0 * flow_rate - cs * cs * inv_solid)
        slope = 2.0 * flow_rate * inv_denom
        csum[j], isol[j], iden[j], slopes[j] = cs, inv_solid, inv_denom, slope
        s_all = slope if s_all is None else s_all * slope
    s_blk[...] = s_all
    for copy in group_copies(0, s_blk, s_rec):
        copy.start()

    take_halo(0)

    lane = lax.broadcasted_iota(jnp.int32, (CHUNK, nz), 1)
    not_last, not_first = lane < nz - 1, lane > 0
    gas_zp = jnp.where(not_last, gas_conduct * 0.25, 0.0)
    gas_zm = jnp.where(not_first, gas_conduct * 0.25, 0.0)
    fx[0:PITCH] = 0.5 * (f0[2, 0:PITCH, :] + f0[2, PITCH:2 * PITCH, :])
    fy[0:8] = 0.5 * (f0[2, PITCH - 8:PITCH, :] + f0[2, PITCH - 7:PITCH + 1, :])

    def chunks(body):
        def step(i, _):
            body(pl.multiple_of(i * CHUNK, CHUNK))
            return 0

        lax.fori_loop(0, rows // CHUNK, step, 0)

    def set_up(at):
        c = f0[2, pl.ds(at + PITCH, CHUNK), :]
        xp = 0.5 * (c + f0[2, pl.ds(at + 2 * PITCH, CHUNK), :])
        xm = 0.5 * (c + f0[2, pl.ds(at, CHUNK), :])
        yp = 0.5 * (c + f0[2, pl.ds(at + PITCH + 1, CHUNK), :])
        ym = 0.5 * (c + f0[2, pl.ds(at + PITCH - 1, CHUNK), :])
        zp = 0.125 * (c + jnp.where(not_last, pltpu.roll(c, nz - 1, 1), 0.0))
        zm = 0.125 * (c + jnp.where(not_first, pltpu.roll(c, 1, 1), 0.0))
        fx[pl.ds(at + PITCH, CHUNK), :] = xp
        fy[pl.ds(at + 8, CHUNK), :] = yp
        fz[pl.ds(at, CHUNK), :] = jnp.where(not_last, zp, 0.0)
        k = c_f[pl.ds(at, CHUNK), :]
        sd = solid_cap + k + (((xp + xm) + (yp + ym)) + (zp + zm))
        gd = (gas_cap + flow_rate + gas_conduct * 2.0 * 2.25) + k
        w = relaxation / (sd * gd - k * k)
        diag[pl.ds(at, CHUNK), :] = sd
        pp[pl.ds(at, CHUNK), :] = gd * w
        qq[pl.ds(at, CHUNK), :] = k * w
        rr[pl.ds(at, CHUNK), :] = sd * w

    chunks(set_up)

    def beside(f, at):
        s = f[0, pl.ds(at + PITCH, CHUNK), :]
        g = f[1, pl.ds(at + PITCH, CHUNK), :]
        z = fz[pl.ds(at, CHUNK), :]
        hs = b_f[0, pl.ds(at, CHUNK), :]
        hs += fx[pl.ds(at + PITCH, CHUNK), :] * f[0, pl.ds(at + 2 * PITCH, CHUNK), :]
        hs += fx[pl.ds(at, CHUNK), :] * f[0, pl.ds(at, CHUNK), :]
        hs += fy[pl.ds(at + 8, CHUNK), :] * f[0, pl.ds(at + PITCH + 1, CHUNK), :]
        hs += fy[pl.ds(at + 7, CHUNK), :] * f[0, pl.ds(at + PITCH - 1, CHUNK), :]
        hs += z * pltpu.roll(s, nz - 1, 1) + pltpu.roll(z * s, 1, 1)
        hg = b_f[1, pl.ds(at, CHUNK), :]
        hg += (flow_rate + gas_conduct) * f[1, pl.ds(at + PITCH - 1, CHUNK), :]
        hg += gas_conduct * (
            f[1, pl.ds(at + PITCH + 1, CHUNK), :]
            + (f[1, pl.ds(at, CHUNK), :] + f[1, pl.ds(at + 2 * PITCH, CHUNK), :]))
        hg += gas_zp * pltpu.roll(g, nz - 1, 1) + gas_zm * pltpu.roll(g, 1, 1)
        return s, g, hs, hg

    def relaxed(f, at):
        s, g, hs, hg = beside(f, at)
        p, q, r = (ref[pl.ds(at, CHUNK), :] for ref in (pp, qq, rr))
        keep = 1.0 - relaxation
        return keep * s + (p * hs + q * hg), keep * g + (q * hs + r * hg)

    def sweep(f, new):
        def body(at):
            new[0, pl.ds(at + PITCH, CHUNK), :], new[1, pl.ds(at + PITCH, CHUNK), :] = relaxed(f, at)

        chunks(body)

    sweep(f0, f1)
    send_halo(1)

    def upstream(d):
        return jnp.full((cx, nz), place, jnp.int32) >= d

    for copy in group_copies(0, s_blk, s_rec):
        copy.wait()
    s_before = s_after = jnp.ones((cx, nz), jnp.float32)
    for d in range(1, group):
        s_d = s_rec[d - 1]
        s_before = jnp.where(upstream(d), s_before * s_d, s_before)
        s_after = jnp.where(upstream(d), s_after, s_after * s_d)
    s_pre[...] = s_before
    s_row[...] = s_before * s_blk[...] * s_after
    for sends, _, copy in row_copies(1, s_row, s_rrec):
        pl.when(sends)(copy.start)

    take_halo(1)
    sweep(f1, f2)
    send_halo(2)
    take_halo(2)

    def residual(at):
        s, g, hs, hg = beside(f2, at)
        k = c_f[pl.ds(at, CHUNK), :]
        gd = (gas_cap + flow_rate + gas_conduct * 2.0 * 2.25) + k
        res[0, pl.ds(at, CHUNK), :] = hs - (diag[pl.ds(at, CHUNK), :] * s - k * g)
        res[1, pl.ds(at, CHUNK), :] = hg - (gd * g - k * s)

    chunks(residual)

    state = jnp.zeros((cx, nz), jnp.float32)
    for j in range(cy):
        r_s = block_sum(lambda at: res[0, at, :], j)
        r_g = block_sum(lambda at: res[1, at, :], j)
        offset = (r_g + csum[j] * r_s * isol[j]) * iden[j]
        cres[j], offs[j] = r_s, offset
        state = slopes[j] * state + offset
    o_blk[...] = state
    for copy in group_copies(2, o_blk, o_rec):
        copy.start()
    for sends, receives, copy in row_copies(1, s_row, s_rrec):
        pl.when(sends)(copy.wait_send)
        pl.when(receives)(copy.wait_recv)
    for copy in group_copies(2, o_blk, o_rec):
        copy.wait()
    state = jnp.zeros((cx, nz), jnp.float32)
    for d in range(group - 1, 0, -1):
        state = jnp.where(upstream(d), s_rec[d - 1] * state + o_rec[d - 1], state)
    before = state
    state = s_blk[...] * state + o_blk[...]
    for d in range(group - 1, 0, -1):
        state = jnp.where(upstream(d), state, s_rec[d - 1] * state + o_rec[d - 1])
    o_row[...] = state
    for sends, _, copy in row_copies(3, o_row, o_rrec):
        pl.when(sends)(copy.start)
    for sends, receives, copy in row_copies(3, o_row, o_rrec):
        pl.when(sends)(copy.wait_send)
        pl.when(receives)(copy.wait_recv)
    state = jnp.zeros((cx, nz), jnp.float32)
    for d in range(n_group - 1, 0, -1):
        state = s_rrec[d - 1] * state + o_rrec[d - 1]
    error = s_pre[...] * state + before
    for j in range(cy):
        error = slopes[j] * error + offs[j]
        solid_error = (cres[j] + csum[j] * error) * isol[j]
        for a in (PITCH, 2 * PITCH):
            for b in (0, 1):
                at = pl.ds(2 * j + a + b, cx, stride=2 * PITCH)
                f3[0, at, :] = f2[0, at, :] + solid_error
                f3[1, at, :] = f2[1, at, :] + error

    send_halo(3)
    take_halo(3)
    sweep(f3, f4)
    send_halo(4)
    take_halo(4)

    def last(i, _):
        s, g = relaxed(f4, pl.multiple_of(i * CHUNK, CHUNK))
        n = CHUNK // PITCH
        for m in range(n):
            o_v[0, i * n + m] = s[m * PITCH:m * PITCH + ny]
            o_v[1, i * n + m] = g[m * PITCH:m * PITCH + ny]
        return 0

    lax.fori_loop(0, rows // CHUNK, last, 0)
    store = pltpu.make_async_copy(o_v, out, in_sem.at[0])
    store.start()
    store.wait()


def shards(n_gx, n_gy, temps, right_side, exchange, coupling):
    _, nx, ny, nz = temps.shape
    group = 8 if n_gy % 8 == 0 else 2
    n_group = n_gy // group
    rows, cx, cy = nx * PITCH, nx // 2, ny // 2
    f32 = jnp.float32
    padded = rows + 2 * PITCH
    kinds = max(group, n_group) - 1
    vmem = lambda *shape: pltpu.VMEM(shape, f32)
    line = lambda *lead: pltpu.VMEM((*lead, cx, nz), f32)
    scratch = [
        vmem(2, nx, ny, nz), vmem(2, nx, ny, nz), vmem(nx, ny, nz), vmem(nx, ny, nz), vmem(2, nx, ny, nz),
        vmem(3, padded, nz), vmem(2, padded, nz), vmem(2, padded, nz), vmem(2, padded, nz), vmem(2, padded, nz),
        vmem(2, rows, nz), vmem(rows, nz),
        vmem(rows + PITCH, nz), vmem(rows + 8, nz), vmem(rows, nz), vmem(rows, nz),
        vmem(rows, nz), vmem(rows, nz), vmem(rows, nz), vmem(2, rows, nz),
        vmem(STAGES, 2, 3, nx, nz), vmem(STAGES, 2, 3, nx, nz),
        line(cy), line(cy), line(cy), line(cy), line(cy), line(cy),
        line(), line(), line(group - 1), line(group - 1),
        line(), line(), line(n_group - 1), line(n_group - 1), line(),
        pltpu.SemaphoreType.DMA((4,)),
        pltpu.SemaphoreType.DMA((STAGES, 4)), pltpu.SemaphoreType.DMA((STAGES, 4)),
        pltpu.SemaphoreType.DMA((4, kinds)), pltpu.SemaphoreType.DMA((4, kinds)),
    ]
    return pl.pallas_call(
        functools.partial(kernel, (nx, ny, nz, n_gx, n_gy, group)),
        out_shape=jax.ShapeDtypeStruct(temps.shape, f32),
        in_specs=[pl.BlockSpec(memory_space=pl.ANY)] * 4,
        out_specs=pl.BlockSpec(memory_space=pl.ANY),
        scratch_shapes=scratch,
        compiler_params=pltpu.CompilerParams(collective_id=0, has_side_effects=True),
    )(temps, right_side, exchange, coupling)


def solution(mesh):
    return jax.shard_map(
        functools.partial(shards, mesh.shape["gx"], mesh.shape["gy"]),
        mesh=mesh,
        in_specs=(
            P(None, "gx", "gy", None),
            P(None, "gx", "gy", None),
            P("gx", "gy", None),
            P("gx", "gy", None),
        ),
        out_specs=P(None, "gx", "gy", None),
        check_vma=False,
    )
```

```python
import functools

import jax
import jax.numpy as jnp
from jax import lax
from jax.experimental import pallas as pl
from jax.experimental.pallas import tpu as pltpu
from jax.sharding import PartitionSpec as P

MESH = pl.DeviceIdType.MESH
EDGE = 8

solid_cap = 0.5
gas_cap = 0.02
flow_rate = 40.0
gas_conduct = 0.05
relaxation = 0.8
lump_factor = 0.25
STAGES = 5


def kernel(dims, temps, right, exch, coup, out, *scratch):
    nx, ny, nz, n_gx, n_gy, group = dims
    pitch = nx + EDGE
    cx, cy = nx // 2, ny // 2
    n_group = n_gy // group
    (e_in, b_f, c_f, o_v, f0, f1, f2, f3, f4, fx, fy, fz, diag, pp, qq, rr, res,
     xs, xr, slopes, csum, isol, iden, cres, offs, s_blk, o_blk, s_rec, o_rec, s_row, o_row, s_rrec, o_rrec, s_pre,
     in_sem, h_send, h_recv, g_send, g_recv) = scratch
    ix, iy = lax.axis_index("gx"), lax.axis_index("gy")
    place, row = lax.rem(iy, group), lax.div(iy, group)

    loads = [
        pltpu.make_async_copy(temps.at[:, pl.ds(y * nx, nx)], f0.at[0:2, pl.ds((y + 1) * pitch, nx)], in_sem.at[3 + y])
        for y in range(ny)
    ]
    loads.append(pltpu.make_async_copy(exch, e_in, in_sem.at[0]))
    more = [pltpu.make_async_copy(coup, c_f, in_sem.at[1]), pltpu.make_async_copy(right, b_f, in_sem.at[2])]
    for load in loads + more:
        load.start()

    barrier = pltpu.get_barrier_semaphore()

    def greet(gx, gy):
        pl.semaphore_signal(barrier, inc=1, device_id=(gx, gy), device_id_type=MESH)

    for d in range(1, group):
        greet(ix, row * group + lax.rem(place + d, group))
    for d in range(1, n_group):
        greet(ix, lax.rem(row + d, n_group) * group + place)
    up_y, down_y, up_x, down_x = iy < n_gy - 1, iy > 0, ix < n_gx - 1, ix > 0
    pl.when(up_y)(lambda: greet(ix, iy + 1))
    pl.when(down_y)(lambda: greet(ix, iy - 1))
    pl.when(up_x)(lambda: greet(ix + 1, iy))
    pl.when(down_x)(lambda: greet(ix - 1, iy))

    fields = (f0, f1, f2, f3, f4)
    plane_zero = jnp.zeros((nx, nz), jnp.float32)
    side_zero = jnp.zeros((ny, nz), jnp.float32)

    def clear_planes(at):
        for f in fields:
            for n in range(f.shape[0]):
                f[n, at:at + nx, :] = plane_zero

    def clear_sides(side):
        for st in range(STAGES):
            for n in range(3 if st == 0 else 2):
                xr[st, side, n] = side_zero

    pl.when(jnp.logical_not(down_y))(lambda: clear_planes(0))
    pl.when(jnp.logical_not(up_y))(lambda: clear_planes((ny + 1) * pitch))
    pl.when(jnp.logical_not(down_x))(lambda: clear_sides(0))
    pl.when(jnp.logical_not(up_x))(lambda: clear_sides(1))
    for d in range(1, n_group):

        @pl.when(row < d)
        def _():
            s_rrec[d - 1] = jnp.ones((cx, nz), jnp.float32)
            o_rrec[d - 1] = jnp.zeros((cx, nz), jnp.float32)

    def halo_copies(st):
        f = fields[st]
        nf = f.shape[0]
        plane = lambda y: f.at[:, (y + 1) * pitch:(y + 1) * pitch + nx]
        parts = (
            (up_y, down_y, plane(ny - 1), plane(-1), (ix, iy + 1)),
            (down_y, up_y, plane(0), plane(ny), (ix, iy - 1)),
            (up_x, down_x, xs.at[st, 1, :nf], xr.at[st, 0, :nf], (ix + 1, iy)),
            (down_x, up_x, xs.at[st, 0, :nf], xr.at[st, 1, :nf], (ix - 1, iy)),
        )
        return [
            (sends, receives, pltpu.make_async_remote_copy(
                src_ref=src, dst_ref=dst, send_sem=h_send.at[st, i], recv_sem=h_recv.at[st, i],
                device_id=to, device_id_type=MESH))
            for i, (sends, receives, src, dst, to) in enumerate(parts)
        ]

    def send_halo(st):
        f = fields[st]
        for n in range(f.shape[0]):
            xs[st, 0, n] = f[n, pl.ds(pitch, ny, stride=pitch), :]
            xs[st, 1, n] = f[n, pl.ds(pitch + nx - 1, ny, stride=pitch), :]
        for sends, _, copy in halo_copies(st):
            pl.when(sends)(copy.start)

    def take_halo(st):
        f = fields[st]
        for sends, receives, copy in halo_copies(st):
            pl.when(sends)(copy.wait_send)
            pl.when(receives)(copy.wait_recv)
        for n in range(f.shape[0]):
            f[n, pl.ds(pitch - 1, ny, stride=pitch), :] = xr[st, 0, n]
            f[n, pl.ds(pitch + nx, ny, stride=pitch), :] = xr[st, 1, n]

    def group_copies(kind, block, received):
        return [
            pltpu.make_async_remote_copy(
                src_ref=block, dst_ref=received.at[d - 1],
                send_sem=g_send.at[kind, d - 1], recv_sem=g_recv.at[kind, d - 1],
                device_id=(ix, row * group + lax.rem(place + d, group)), device_id_type=MESH)
            for d in range(1, group)
        ]

    def row_copies(kind, block, received):
        return [
            (row + d < n_group, row >= d, pltpu.make_async_remote_copy(
                src_ref=block, dst_ref=received.at[d - 1],
                send_sem=g_send.at[kind, d - 1], recv_sem=g_recv.at[kind, d - 1],
                device_id=(ix, (row + d) * group + place), device_id_type=MESH))
            for d in range(1, n_group)
        ]

    def planes(body, unroll=2):
        def step(y, _):
            body(y, pl.multiple_of(y * nx, 8), pl.multiple_of((y + 1) * pitch, 8))
            return 0

        lax.fori_loop(0, ny, step, 0, unroll=unroll)

    def conductivity(y, at, on):
        t = f0[0, pl.ds(on, nx), :]
        f0[2, pl.ds(on, nx), :] = 1.0 + 4.0 * e_in[pl.ds(at, nx), :] * (t * t * t)

    for load in loads:
        load.wait()
    planes(conductivity)
    n_halo = sum(v.astype(jnp.int32) for v in (up_y, down_y, up_x, down_x))
    pl.semaphore_wait(barrier, (group - 1) + (n_group - 1) + n_halo)
    send_halo(0)
    for load in more:
        load.wait()

    def block_sum(load, j, step):
        total = None
        for a in (0, step):
            for b in (0, 1):
                part = load(pl.ds(2 * j * step + a + b, cx, stride=2))
                total = part if total is None else total + part
        return total

    s_all = None
    for j in range(cy):
        cs = block_sum(lambda at: c_f[at, :], j, nx)
        cond = block_sum(lambda at: f0[2, pl.ds(at.start + pitch, at.size, stride=at.stride), :], j, pitch)
        inv_solid = 1.0 / (4.0 * solid_cap + cs + lump_factor * cond)
        inv_denom = 1.0 / (4.0 * gas_cap + cs + 2.0 * flow_rate - cs * cs * inv_solid)
        slope = 2.0 * flow_rate * inv_denom
        csum[j], isol[j], iden[j], slopes[j] = cs, inv_solid, inv_denom, slope
        s_all = slope if s_all is None else s_all * slope
    s_blk[...] = s_all
    for copy in group_copies(0, s_blk, s_rec):
        copy.start()

    take_halo(0)

    lane = lax.broadcasted_iota(jnp.int32, (nx, nz), 1)
    not_last, not_first = lane < nz - 1, lane > 0
    gas_zp = jnp.where(not_last, gas_conduct * 0.25, 0.0)
    gas_zm = jnp.where(not_first, gas_conduct * 0.25, 0.0)
    fy[0:nx] = 0.5 * (f0[2, 0:nx, :] + f0[2, pitch:pitch + nx, :])

    def set_up(y, at, on):
        c = f0[2, pl.ds(on, nx), :]
        xp = 0.5 * (c + f0[2, pl.ds(on + 1, nx), :])
        xm = 0.5 * (c + f0[2, pl.ds(on - 1, nx), :])
        yp = 0.5 * (c + f0[2, pl.ds(on + pitch, nx), :])
        ym = 0.5 * (c + f0[2, pl.ds(on - pitch, nx), :])
        zp = 0.125 * (c + jnp.where(not_last, pltpu.roll(c, nz - 1, 1), 0.0))
        zm = 0.125 * (c + jnp.where(not_first, pltpu.roll(c, 1, 1), 0.0))
        fx[pl.ds(on, nx), :] = xp
        fx[pl.ds(on - 8, 8), :] = 0.5 * (f0[2, pl.ds(on - 8, 8), :] + f0[2, pl.ds(on - 7, 8), :])
        fy[pl.ds(at + nx, nx), :] = yp
        fz[pl.ds(at, nx), :] = jnp.where(not_last, zp, 0.0)
        k = c_f[pl.ds(at, nx), :]
        sd = solid_cap + k + (((xp + xm) + (yp + ym)) + (zp + zm))
        gd = (gas_cap + flow_rate + gas_conduct * 2.0 * 2.25) + k
        w = relaxation / (sd * gd - k * k)
        diag[pl.ds(at, nx), :] = sd
        pp[pl.ds(at, nx), :] = gd * w
        qq[pl.ds(at, nx), :] = k * w
        rr[pl.ds(at, nx), :] = sd * w

    planes(set_up)

    def beside(f, at, on):
        s = f[0, pl.ds(on, nx), :]
        g = f[1, pl.ds(on, nx), :]
        z = fz[pl.ds(at, nx), :]
        hs = b_f[0, pl.ds(at, nx), :]
        hs += fy[pl.ds(at + nx, nx), :] * f[0, pl.ds(on + pitch, nx), :]
        hs += fy[pl.ds(at, nx), :] * f[0, pl.ds(on - pitch, nx), :]
        hs += fx[pl.ds(on, nx), :] * f[0, pl.ds(on + 1, nx), :]
        hs += fx[pl.ds(on - 1, nx), :] * f[0, pl.ds(on - 1, nx), :]
        hs += z * pltpu.roll(s, nz - 1, 1) + pltpu.roll(z * s, 1, 1)
        hg = b_f[1, pl.ds(at, nx), :]
        hg += (flow_rate + gas_conduct) * f[1, pl.ds(on - pitch, nx), :]
        hg += gas_conduct * (
            f[1, pl.ds(on + pitch, nx), :]
            + (f[1, pl.ds(on - 1, nx), :] + f[1, pl.ds(on + 1, nx), :]))
        hg += gas_zp * pltpu.roll(g, nz - 1, 1) + gas_zm * pltpu.roll(g, 1, 1)
        return s, g, hs, hg

    def relaxed(f, at, on):
        s, g, hs, hg = beside(f, at, on)
        p, q, r = (ref[pl.ds(at, nx), :] for ref in (pp, qq, rr))
        keep = 1.0 - relaxation
        return keep * s + (p * hs + q * hg), keep * g + (q * hs + r * hg)

    def sweep(f, new):
        def body(y, at, on):
            new[0, pl.ds(on, nx), :], new[1, pl.ds(on, nx), :] = relaxed(f, at, on)

        planes(body)

    sweep(f0, f1)
    send_halo(1)

    def upstream(d):
        return jnp.full((cx, nz), place, jnp.int32) >= d

    for copy in group_copies(0, s_blk, s_rec):
        copy.wait()
    s_before = s_after = jnp.ones((cx, nz), jnp.float32)
    for d in range(1, group):
        s_d = s_rec[d - 1]
        s_before = jnp.where(upstream(d), s_before * s_d, s_before)
        s_after = jnp.where(upstream(d), s_after, s_after * s_d)
    s_pre[...] = s_before
    s_row[...] = s_before * s_blk[...] * s_after
    for sends, _, copy in row_copies(1, s_row, s_rrec):
        pl.when(sends)(copy.start)

    take_halo(1)
    sweep(f1, f2)
    send_halo(2)
    take_halo(2)

    def residual(y, at, on):
        s, g, hs, hg = beside(f2, at, on)
        k = c_f[pl.ds(at, nx), :]
        gd = (gas_cap + flow_rate + gas_conduct * 2.0 * 2.25) + k
        res[0, pl.ds(at, nx), :] = hs - (diag[pl.ds(at, nx), :] * s - k * g)
        res[1, pl.ds(at, nx), :] = hg - (gd * g - k * s)

    planes(residual)

    state = jnp.zeros((cx, nz), jnp.float32)
    for j in range(cy):
        r_s = block_sum(lambda at: res[0, at, :], j, nx)
        r_g = block_sum(lambda at: res[1, at, :], j, nx)
        offset = (r_g + csum[j] * r_s * isol[j]) * iden[j]
        cres[j], offs[j] = r_s, offset
        state = slopes[j] * state + offset
    o_blk[...] = state
    for copy in group_copies(2, o_blk, o_rec):
        copy.start()
    for sends, receives, copy in row_copies(1, s_row, s_rrec):
        pl.when(sends)(copy.wait_send)
        pl.when(receives)(copy.wait_recv)
    for copy in group_copies(2, o_blk, o_rec):
        copy.wait()
    state = jnp.zeros((cx, nz), jnp.float32)
    for d in range(group - 1, 0, -1):
        state = jnp.where(upstream(d), s_rec[d - 1] * state + o_rec[d - 1], state)
    before = state
    state = s_blk[...] * state + o_blk[...]
    for d in range(group - 1, 0, -1):
        state = jnp.where(upstream(d), state, s_rec[d - 1] * state + o_rec[d - 1])
    o_row[...] = state
    for sends, _, copy in row_copies(3, o_row, o_rrec):
        pl.when(sends)(copy.start)
    for sends, receives, copy in row_copies(3, o_row, o_rrec):
        pl.when(sends)(copy.wait_send)
        pl.when(receives)(copy.wait_recv)
    state = jnp.zeros((cx, nz), jnp.float32)
    for d in range(n_group - 1, 0, -1):
        state = s_rrec[d - 1] * state + o_rrec[d - 1]
    error = s_pre[...] * state + before
    for j in range(cy):
        error = slopes[j] * error + offs[j]
        solid_error = (cres[j] + csum[j] * error) * isol[j]
        for a in (pitch, 2 * pitch):
            for b in (0, 1):
                at = pl.ds(2 * j * pitch + a + b, cx, stride=2)
                f3[0, at, :] = f2[0, at, :] + solid_error
                f3[1, at, :] = f2[1, at, :] + error

    send_halo(3)
    take_halo(3)
    sweep(f3, f4)
    send_halo(4)
    take_halo(4)

    def last(y, at, on):
        o_v[0, pl.ds(at, nx), :], o_v[1, pl.ds(at, nx), :] = relaxed(f4, at, on)

    planes(last)
    store = pltpu.make_async_copy(o_v, out, in_sem.at[0])
    store.start()
    store.wait()


def shards(n_gx, n_gy, temps, right_side, exchange, coupling):
    _, nx, ny, nz = temps.shape
    group = 8 if n_gy % 8 == 0 else 2
    n_group = n_gy // group
    rows, cx, cy = nx * ny, nx // 2, ny // 2
    f32 = jnp.float32
    padded = (nx + EDGE) * (ny + 2)
    kinds = max(group, n_group) - 1
    vmem = lambda *shape: pltpu.VMEM(shape, f32)
    line = lambda *lead: pltpu.VMEM((*lead, cx, nz), f32)
    scratch = [
        vmem(rows, nz), vmem(2, rows, nz), vmem(rows, nz), vmem(2, rows, nz),
        vmem(3, padded, nz), vmem(2, padded, nz), vmem(2, padded, nz), vmem(2, padded, nz), vmem(2, padded, nz),
        vmem(padded, nz), vmem(rows + nx, nz), vmem(rows, nz), vmem(rows, nz),
        vmem(rows, nz), vmem(rows, nz), vmem(rows, nz), vmem(2, rows, nz),
        vmem(STAGES, 2, 3, ny, nz), vmem(STAGES, 2, 3, ny, nz),
        line(cy), line(cy), line(cy), line(cy), line(cy), line(cy),
        line(), line(), line(group - 1), line(group - 1),
        line(), line(), line(n_group - 1), line(n_group - 1), line(),
        pltpu.SemaphoreType.DMA((3 + ny,)),
        pltpu.SemaphoreType.DMA((STAGES, 4)), pltpu.SemaphoreType.DMA((STAGES, 4)),
        pltpu.SemaphoreType.DMA((4, kinds)), pltpu.SemaphoreType.DMA((4, kinds)),
    ]
    flat = lambda a: jnp.swapaxes(a, -3, -2).reshape(*a.shape[:-3], rows, nz)
    out = pl.pallas_call(
        functools.partial(kernel, (nx, ny, nz, n_gx, n_gy, group)),
        out_shape=jax.ShapeDtypeStruct((2, rows, nz), f32),
        in_specs=[pl.BlockSpec(memory_space=pl.ANY)] * 4,
        out_specs=pl.BlockSpec(memory_space=pl.ANY),
        scratch_shapes=scratch,
        compiler_params=pltpu.CompilerParams(collective_id=0, has_side_effects=True),
    )(flat(temps), flat(right_side), flat(exchange), flat(coupling))
    return jnp.swapaxes(out.reshape(2, ny, nx, nz), 1, 2)


def solution(mesh):
    return jax.shard_map(
        functools.partial(shards, mesh.shape["gx"], mesh.shape["gy"]),
        mesh=mesh,
        in_specs=(
            P(None, "gx", "gy", None),
            P(None, "gx", "gy", None),
            P("gx", "gy", None),
            P("gx", "gy", None),
        ),
        out_specs=P(None, "gx", "gy", None),
        check_vma=False,
    )
```

```python
import functools

import jax
import jax.numpy as jnp
from jax import lax
from jax.experimental import pallas as pl
from jax.experimental.pallas import tpu as pltpu
from jax.sharding import PartitionSpec as P

MESH = pl.DeviceIdType.MESH
EDGE = 8

solid_cap = 0.5
gas_cap = 0.02
flow_rate = 40.0
gas_conduct = 0.05
relaxation = 0.8
lump_factor = 0.25
STAGES = 5


class Cells:
    def __init__(self, at, on, n, step=None, skip=None):
        self.at, self.on, self.n, self.step, self.skip = at, on, n, step, skip

    def coef(self, shift=0):
        return pl.ds(self.at + shift, self.n, stride=self.step)

    def field(self, shift=0):
        return pl.ds(self.on + shift, self.n, stride=self.skip)


def kernel(dims, temps, right, exch, coup, out, *scratch):
    nx, ny, nz, n_gx, n_gy, group = dims
    pitch = nx + EDGE
    cx, cy = nx // 2, ny // 2
    n_group = n_gy // group
    (e_in, b_f, c_f, o_v, f0, f1, f2, f3, f4, fx, fy, fz, diag, pp, qq, rr, res,
     xs, xr, slopes, csum, isol, iden, cres, offs, s_blk, o_blk, s_rec, o_rec, s_row, o_row, s_rrec, o_rrec, s_pre,
     in_sem, h_send, h_recv, g_send, g_recv) = scratch
    ix, iy = lax.axis_index("gx"), lax.axis_index("gy")
    place, row = lax.rem(iy, group), lax.div(iy, group)

    loads = [
        pltpu.make_async_copy(temps.at[:, pl.ds(y * nx, nx)], f0.at[0:2, pl.ds((y + 1) * pitch, nx)], in_sem.at[3 + y])
        for y in range(ny)
    ]
    loads.append(pltpu.make_async_copy(exch, e_in, in_sem.at[0]))
    more = [pltpu.make_async_copy(coup, c_f, in_sem.at[1]), pltpu.make_async_copy(right, b_f, in_sem.at[2])]
    for load in loads + more:
        load.start()

    barrier = pltpu.get_barrier_semaphore()

    def greet(gx, gy):
        pl.semaphore_signal(barrier, inc=1, device_id=(gx, gy), device_id_type=MESH)

    for d in range(1, group):
        greet(ix, row * group + lax.rem(place + d, group))
    for d in range(1, n_group):
        greet(ix, lax.rem(row + d, n_group) * group + place)
    up_y, down_y, up_x, down_x = iy < n_gy - 1, iy > 0, ix < n_gx - 1, ix > 0
    pl.when(up_y)(lambda: greet(ix, iy + 1))
    pl.when(down_y)(lambda: greet(ix, iy - 1))
    pl.when(up_x)(lambda: greet(ix + 1, iy))
    pl.when(down_x)(lambda: greet(ix - 1, iy))

    fields = (f0, f1, f2, f3, f4)
    plane_zero = jnp.zeros((nx, nz), jnp.float32)
    side_zero = jnp.zeros((ny, nz), jnp.float32)

    def clear_planes(at):
        for f in fields:
            for n in range(f.shape[0]):
                f[n, at:at + nx, :] = plane_zero

    def clear_sides(side):
        for st in range(STAGES):
            for n in range(3 if st == 0 else 2):
                xr[st, side, n] = side_zero

    pl.when(jnp.logical_not(down_y))(lambda: clear_planes(0))
    pl.when(jnp.logical_not(up_y))(lambda: clear_planes((ny + 1) * pitch))
    pl.when(jnp.logical_not(down_x))(lambda: clear_sides(0))
    pl.when(jnp.logical_not(up_x))(lambda: clear_sides(1))
    for d in range(1, n_group):

        @pl.when(row < d)
        def _():
            s_rrec[d - 1] = jnp.ones((cx, nz), jnp.float32)
            o_rrec[d - 1] = jnp.zeros((cx, nz), jnp.float32)

    def halo_copies(st):
        f = fields[st]
        nf = f.shape[0]
        plane = lambda y: f.at[:, (y + 1) * pitch:(y + 1) * pitch + nx]
        parts = (
            (up_y, down_y, plane(ny - 1), plane(-1), (ix, iy + 1)),
            (down_y, up_y, plane(0), plane(ny), (ix, iy - 1)),
            (up_x, down_x, xs.at[st, 1, :nf], xr.at[st, 0, :nf], (ix + 1, iy)),
            (down_x, up_x, xs.at[st, 0, :nf], xr.at[st, 1, :nf], (ix - 1, iy)),
        )
        return [
            (sends, receives, pltpu.make_async_remote_copy(
                src_ref=src, dst_ref=dst, send_sem=h_send.at[st, i], recv_sem=h_recv.at[st, i],
                device_id=to, device_id_type=MESH))
            for i, (sends, receives, src, dst, to) in enumerate(parts)
        ]

    def send_halo(st):
        f = fields[st]
        for n in range(f.shape[0]):
            xs[st, 0, n] = f[n, pl.ds(pitch, ny, stride=pitch), :]
            xs[st, 1, n] = f[n, pl.ds(pitch + nx - 1, ny, stride=pitch), :]
        for sends, _, copy in halo_copies(st):
            pl.when(sends)(copy.start)

    def take_halo(st):
        f = fields[st]
        for sends, receives, copy in halo_copies(st):
            pl.when(sends)(copy.wait_send)
            pl.when(receives)(copy.wait_recv)
        for n in range(f.shape[0]):
            f[n, pl.ds(pitch - 1, ny, stride=pitch), :] = xr[st, 0, n]
            f[n, pl.ds(pitch + nx, ny, stride=pitch), :] = xr[st, 1, n]

    def group_copies(kind, block, received):
        return [
            pltpu.make_async_remote_copy(
                src_ref=block, dst_ref=received.at[d - 1],
                send_sem=g_send.at[kind, d - 1], recv_sem=g_recv.at[kind, d - 1],
                device_id=(ix, row * group + lax.rem(place + d, group)), device_id_type=MESH)
            for d in range(1, group)
        ]

    def row_copies(kind, block, received):
        return [
            (row + d < n_group, row >= d, pltpu.make_async_remote_copy(
                src_ref=block, dst_ref=received.at[d - 1],
                send_sem=g_send.at[kind, d - 1], recv_sem=g_recv.at[kind, d - 1],
                device_id=(ix, (row + d) * group + place), device_id_type=MESH))
            for d in range(1, n_group)
        ]

    def plane(y):
        return Cells(y * nx, (y + 1) * pitch, nx)

    def inner(body, low=1, high=ny - 1, unroll=2):
        def step(y, _):
            body(Cells(pl.multiple_of(y * nx, 8), pl.multiple_of((y + 1) * pitch, 8), nx))
            return 0

        lax.fori_loop(low, high, step, 0, unroll=unroll)

    def outer(body):
        for y in (0, ny - 1):
            body(plane(y))
        for x in (0, nx - 1):
            body(Cells(x, pitch + x, ny, nx, pitch))

    def conductivity(u):
        t = f0[0, u.field(), :]
        f0[2, u.field(), :] = 1.0 + 4.0 * e_in[u.coef(), :] * (t * t * t)

    for load in loads:
        load.wait()
    inner(conductivity, 0, ny)
    n_halo = sum(v.astype(jnp.int32) for v in (up_y, down_y, up_x, down_x))
    pl.semaphore_wait(barrier, (group - 1) + (n_group - 1) + n_halo)
    send_halo(0)
    for load in more:
        load.wait()

    def block_sum(load, j, step):
        total = None
        for a in (0, step):
            for b in (0, 1):
                part = load(pl.ds(2 * j * step + a + b, cx, stride=2))
                total = part if total is None else total + part
        return total

    s_all = None
    for j in range(cy):
        cs = block_sum(lambda at: c_f[at, :], j, nx)
        cond = block_sum(lambda at: f0[2, pl.ds(at.start + pitch, at.size, stride=at.stride), :], j, pitch)
        inv_solid = 1.0 / (4.0 * solid_cap + cs + lump_factor * cond)
        inv_denom = 1.0 / (4.0 * gas_cap + cs + 2.0 * flow_rate - cs * cs * inv_solid)
        slope = 2.0 * flow_rate * inv_denom
        csum[j], isol[j], iden[j], slopes[j] = cs, inv_solid, inv_denom, slope
        s_all = slope if s_all is None else s_all * slope
    s_blk[...] = s_all
    for copy in group_copies(0, s_blk, s_rec):
        copy.start()

    lane = lax.broadcasted_iota(jnp.int32, (1, nz), 1)
    not_last = (lane < nz - 1).astype(jnp.float32)
    not_first = (lane > 0).astype(jnp.float32)
    gas_zp = gas_conduct * 0.25 * not_last
    gas_zm = gas_conduct * 0.25 * not_first

    def set_up(u):
        c = f0[2, u.field(), :]
        xp = 0.5 * (c + f0[2, u.field(1), :])
        xm = 0.5 * (c + f0[2, u.field(-1), :])
        yp = 0.5 * (c + f0[2, u.field(pitch), :])
        ym = 0.5 * (c + f0[2, u.field(-pitch), :])
        zp = 0.125 * (c + not_last * pltpu.roll(c, nz - 1, 1))
        zm = 0.125 * (c + not_first * pltpu.roll(c, 1, 1))
        fx[u.field(), :] = xp
        if u.step is None:
            fx[pl.ds(u.on - 8, 8), :] = 0.5 * (f0[2, pl.ds(u.on - 8, 8), :] + f0[2, pl.ds(u.on - 7, 8), :])
        else:
            fx[u.field(-1), :] = xm
        fy[u.coef(), :] = ym
        fy[u.coef(nx), :] = yp
        fz[u.coef(), :] = not_last * zp
        k = c_f[u.coef(), :]
        sd = solid_cap + k + (((xp + xm) + (yp + ym)) + (zp + zm))
        gd = (gas_cap + flow_rate + gas_conduct * 2.0 * 2.25) + k
        w = relaxation / (sd * gd - k * k)
        diag[u.coef(), :] = sd
        pp[u.coef(), :] = gd * w
        qq[u.coef(), :] = k * w
        rr[u.coef(), :] = sd * w

    def beside(f, u):
        s = f[0, u.field(), :]
        g = f[1, u.field(), :]
        z = fz[u.coef(), :]
        hs = b_f[0, u.coef(), :]
        hs += fy[u.coef(nx), :] * f[0, u.field(pitch), :]
        hs += fy[u.coef(), :] * f[0, u.field(-pitch), :]
        hs += fx[u.field(), :] * f[0, u.field(1), :]
        hs += fx[u.field(-1), :] * f[0, u.field(-1), :]
        hs += z * pltpu.roll(s, nz - 1, 1) + pltpu.roll(z * s, 1, 1)
        hg = b_f[1, u.coef(), :]
        hg += (flow_rate + gas_conduct) * f[1, u.field(-pitch), :]
        hg += gas_conduct * (f[1, u.field(pitch), :] + (f[1, u.field(-1), :] + f[1, u.field(1), :]))
        hg += gas_zp * pltpu.roll(g, nz - 1, 1) + gas_zm * pltpu.roll(g, 1, 1)
        return s, g, hs, hg

    def relaxed(f, u):
        s, g, hs, hg = beside(f, u)
        p, q, r = pp[u.coef(), :], qq[u.coef(), :], rr[u.coef(), :]
        keep = 1.0 - relaxation
        return keep * s + (p * hs + q * hg), keep * g + (q * hs + r * hg)

    def sweep(f, new):
        def body(u):
            new[0, u.field(), :], new[1, u.field(), :] = relaxed(f, u)

        return body

    inner(set_up)
    inner(sweep(f0, f1))
    take_halo(0)
    outer(set_up)
    outer(sweep(f0, f1))
    send_halo(1)
    inner(sweep(f1, f2))

    def upstream(d):
        return jnp.full((cx, nz), place, jnp.int32) >= d

    for copy in group_copies(0, s_blk, s_rec):
        copy.wait()
    s_before = s_after = jnp.ones((cx, nz), jnp.float32)
    for d in range(1, group):
        s_d = s_rec[d - 1]
        s_before = jnp.where(upstream(d), s_before * s_d, s_before)
        s_after = jnp.where(upstream(d), s_after, s_after * s_d)
    s_pre[...] = s_before
    s_row[...] = s_before * s_blk[...] * s_after
    for sends, _, copy in row_copies(1, s_row, s_rrec):
        pl.when(sends)(copy.start)

    take_halo(1)
    outer(sweep(f1, f2))
    send_halo(2)

    def residual(u):
        s, g, hs, hg = beside(f2, u)
        k = c_f[u.coef(), :]
        gd = (gas_cap + flow_rate + gas_conduct * 2.0 * 2.25) + k
        res[0, u.coef(), :] = hs - (diag[u.coef(), :] * s - k * g)
        res[1, u.coef(), :] = hg - (gd * g - k * s)

    inner(residual)
    take_halo(2)
    outer(residual)

    state = jnp.zeros((cx, nz), jnp.float32)
    for j in range(cy):
        r_s = block_sum(lambda at: res[0, at, :], j, nx)
        r_g = block_sum(lambda at: res[1, at, :], j, nx)
        offset = (r_g + csum[j] * r_s * isol[j]) * iden[j]
        cres[j], offs[j] = r_s, offset
        state = slopes[j] * state + offset
    o_blk[...] = state
    for copy in group_copies(2, o_blk, o_rec):
        copy.start()
    for sends, receives, copy in row_copies(1, s_row, s_rrec):
        pl.when(sends)(copy.wait_send)
        pl.when(receives)(copy.wait_recv)
    for copy in group_copies(2, o_blk, o_rec):
        copy.wait()
    state = jnp.zeros((cx, nz), jnp.float32)
    for d in range(group - 1, 0, -1):
        state = jnp.where(upstream(d), s_rec[d - 1] * state + o_rec[d - 1], state)
    before = state
    state = s_blk[...] * state + o_blk[...]
    for d in range(group - 1, 0, -1):
        state = jnp.where(upstream(d), state, s_rec[d - 1] * state + o_rec[d - 1])
    o_row[...] = state
    for sends, _, copy in row_copies(3, o_row, o_rrec):
        pl.when(sends)(copy.start)
    for sends, receives, copy in row_copies(3, o_row, o_rrec):
        pl.when(sends)(copy.wait_send)
        pl.when(receives)(copy.wait_recv)
    state = jnp.zeros((cx, nz), jnp.float32)
    for d in range(n_group - 1, 0, -1):
        state = s_rrec[d - 1] * state + o_rrec[d - 1]
    error = s_pre[...] * state + before
    for j in range(cy):
        error = slopes[j] * error + offs[j]
        solid_error = (cres[j] + csum[j] * error) * isol[j]
        for a in (pitch, 2 * pitch):
            for b in (0, 1):
                at = pl.ds(2 * j * pitch + a + b, cx, stride=2)
                f3[0, at, :] = f2[0, at, :] + solid_error
                f3[1, at, :] = f2[1, at, :] + error

    def last(u):
        o_v[0, u.coef(), :], o_v[1, u.coef(), :] = relaxed(f4, u)

    send_halo(3)
    inner(sweep(f3, f4))
    take_halo(3)
    outer(sweep(f3, f4))
    send_halo(4)
    inner(last)
    take_halo(4)
    outer(last)
    store = pltpu.make_async_copy(o_v, out, in_sem.at[0])
    store.start()
    store.wait()


def shards(n_gx, n_gy, temps, right_side, exchange, coupling):
    _, nx, ny, nz = temps.shape
    group = 8 if n_gy % 8 == 0 else 2
    n_group = n_gy // group
    rows, cx, cy = nx * ny, nx // 2, ny // 2
    f32 = jnp.float32
    padded = (nx + EDGE) * (ny + 2)
    kinds = max(group, n_group) - 1
    vmem = lambda *shape: pltpu.VMEM(shape, f32)
    line = lambda *lead: pltpu.VMEM((*lead, cx, nz), f32)
    scratch = [
        vmem(rows, nz), vmem(2, rows, nz), vmem(rows, nz), vmem(2, rows, nz),
        vmem(3, padded, nz), vmem(2, padded, nz), vmem(2, padded, nz), vmem(2, padded, nz), vmem(2, padded, nz),
        vmem(padded, nz), vmem(rows + nx, nz), vmem(rows, nz), vmem(rows, nz),
        vmem(rows, nz), vmem(rows, nz), vmem(rows, nz), vmem(2, rows, nz),
        vmem(STAGES, 2, 3, ny, nz), vmem(STAGES, 2, 3, ny, nz),
        line(cy), line(cy), line(cy), line(cy), line(cy), line(cy),
        line(), line(), line(group - 1), line(group - 1),
        line(), line(), line(n_group - 1), line(n_group - 1), line(),
        pltpu.SemaphoreType.DMA((3 + ny,)),
        pltpu.SemaphoreType.DMA((STAGES, 4)), pltpu.SemaphoreType.DMA((STAGES, 4)),
        pltpu.SemaphoreType.DMA((4, kinds)), pltpu.SemaphoreType.DMA((4, kinds)),
    ]
    flat = lambda a: jnp.swapaxes(a, -3, -2).reshape(*a.shape[:-3], rows, nz)
    out = pl.pallas_call(
        functools.partial(kernel, (nx, ny, nz, n_gx, n_gy, group)),
        out_shape=jax.ShapeDtypeStruct((2, rows, nz), f32),
        in_specs=[pl.BlockSpec(memory_space=pl.ANY)] * 4,
        out_specs=pl.BlockSpec(memory_space=pl.ANY),
        scratch_shapes=scratch,
        compiler_params=pltpu.CompilerParams(collective_id=0, has_side_effects=True),
    )(flat(temps), flat(right_side), flat(exchange), flat(coupling))
    return jnp.swapaxes(out.reshape(2, ny, nx, nz), 1, 2)


def solution(mesh):
    return jax.shard_map(
        functools.partial(shards, mesh.shape["gx"], mesh.shape["gy"]),
        mesh=mesh,
        in_specs=(
            P(None, "gx", "gy", None),
            P(None, "gx", "gy", None),
            P("gx", "gy", None),
            P("gx", "gy", None),
        ),
        out_specs=P(None, "gx", "gy", None),
        check_vma=False,
    )
```

```python
import functools

import jax
import jax.numpy as jnp
from jax import lax
from jax.experimental import pallas as pl
from jax.experimental.pallas import tpu as pltpu
from jax.sharding import PartitionSpec as P

MESH = pl.DeviceIdType.MESH
EDGE = 8

solid_cap = 0.5
gas_cap = 0.02
flow_rate = 40.0
gas_conduct = 0.05
relaxation = 0.8
lump_factor = 0.25
STAGES = 5


class Cells:
    def __init__(self, at, on, n, step=None, skip=None):
        self.at, self.on, self.n, self.step, self.skip = at, on, n, step, skip

    def coef(self, shift=0):
        return pl.ds(self.at + shift, self.n, stride=self.step)

    def field(self, shift=0):
        return pl.ds(self.on + shift, self.n, stride=self.skip)


def kernel(dims, temps, right, exch, coup, out, *scratch):
    nx, ny, nz, n_gx, n_gy, group = dims
    pitch = nx + EDGE
    cx, cy = nx // 2, ny // 2
    n_group = n_gy // group
    (e_in, c_f, o_v, f0, f1, f2, f3, f4, cf, fx, fy, diag, res, xs, xr, xs3, xr3, coarse,
     s_blk, o_blk, s_rec, o_rec, s_row, o_row, s_rrec, o_rrec, s_pre,
     in_sem, h_send, h_recv, w_send, w_recv, g_send, g_recv) = scratch
    P_, Q_, R_, FZ, B_S, B_G = range(6)
    CSUM, ISOL, CRES, SLOPE, OFFS = range(5)
    own = slice(nx, (ny + 1) * nx)
    first_on = 2 * pitch
    ix, iy = lax.axis_index("gx"), lax.axis_index("gy")
    place, row = lax.rem(iy, group), lax.div(iy, group)

    loads = [
        pltpu.make_async_copy(temps.at[:, pl.ds(y * nx, nx)], f0.at[0:2, pl.ds((y + 2) * pitch, nx)], in_sem.at[3 + y])
        for y in range(ny)
    ]
    loads.append(pltpu.make_async_copy(exch, e_in.at[own], in_sem.at[0]))
    more = [pltpu.make_async_copy(coup, c_f.at[own], in_sem.at[1]), pltpu.make_async_copy(right, cf.at[B_S:B_G + 1, own], in_sem.at[2])]
    for load in loads + more:
        load.start()

    barrier = pltpu.get_barrier_semaphore()

    def greet(gx, gy):
        pl.semaphore_signal(barrier, inc=1, device_id=(gx, gy), device_id_type=MESH)

    for d in range(1, group):
        greet(ix, row * group + lax.rem(place + d, group))
    for d in range(1, n_group):
        greet(ix, lax.rem(row + d, n_group) * group + place)
    up_y, down_y, up_x, down_x = iy < n_gy - 1, iy > 0, ix < n_gx - 1, ix > 0
    pl.when(up_y)(lambda: greet(ix, iy + 1))
    pl.when(down_y)(lambda: greet(ix, iy - 1))
    pl.when(up_x)(lambda: greet(ix + 1, iy))
    pl.when(down_x)(lambda: greet(ix - 1, iy))

    fields = (f0, f1, f2, f3, f4)
    plane_zero = jnp.zeros((nx, nz), jnp.float32)
    side_zero = jnp.zeros((ny, nz), jnp.float32)

    def clear_planes(y, far, face, line):
        for f in fields:
            for n in range(f.shape[0]):
                f[n, (y + 2) * pitch:(y + 2) * pitch + nx, :] = plane_zero
        for n in range(2):
            f2[n, (far + 2) * pitch:(far + 2) * pitch + nx, :] = plane_zero
        for n in range(6):
            cf[n, (y + 1) * nx:(y + 2) * nx, :] = plane_zero
        fx[(y + 2) * pitch - 8:(y + 2) * pitch + nx, :] = jnp.zeros((nx + 8, nz), jnp.float32)
        fy[face * nx:(face + 1) * nx, :] = plane_zero
        for n in range(5):
            coarse[n, line] = jnp.zeros((cx, nz), jnp.float32)

    def clear_sides(side):
        for st in range(STAGES):
            for n in range(3 if st == 0 else 2):
                xr[st, side, n] = side_zero
        for n in range(2):
            xr3[side, n] = jnp.zeros((ny + 2, nz), jnp.float32)

    pl.when(jnp.logical_not(down_y))(lambda: clear_planes(-1, -2, 0, 0))
    pl.when(jnp.logical_not(up_y))(lambda: clear_planes(ny, ny + 1, ny + 2, cy + 1))
    pl.when(jnp.logical_not(down_x))(lambda: clear_sides(0))
    pl.when(jnp.logical_not(up_x))(lambda: clear_sides(1))
    for d in range(1, n_group):

        @pl.when(row < d)
        def _():
            s_rrec[d - 1] = jnp.ones((cx, nz), jnp.float32)
            o_rrec[d - 1] = jnp.zeros((cx, nz), jnp.float32)

    def remote(src, dst, send, recv, to):
        return pltpu.make_async_remote_copy(
            src_ref=src, dst_ref=dst, send_sem=send, recv_sem=recv, device_id=to, device_id_type=MESH)

    def halo_copies(st):
        f = fields[st]
        nf = f.shape[0]
        plane = lambda y: f.at[:, (y + 2) * pitch:(y + 2) * pitch + nx]
        sides = (xs3, xr3) if st == 3 else (xs.at[st, :, :nf], xr.at[st, :, :nf])
        parts = [
            (up_x, down_x, sides[0].at[1], sides[1].at[0], (ix + 1, iy)),
            (down_x, up_x, sides[0].at[0], sides[1].at[1], (ix - 1, iy)),
        ]
        if st < 3:
            parts += [
                (up_y, down_y, plane(ny - 1), plane(-1), (ix, iy + 1)),
                (down_y, up_y, plane(0), plane(ny), (ix, iy - 1)),
            ]
        return [
            (sends, receives, remote(src, dst, h_send.at[st, i], h_recv.at[st, i], to))
            for i, (sends, receives, src, dst, to) in enumerate(parts)
        ]

    def side_rows(st, x):
        more = 1 if st == 3 else 0
        return pl.ds(first_on - more * pitch + x, ny + 2 * more, stride=pitch)

    def send_halo(st):
        f = fields[st]
        for n in range(f.shape[0]):
            for side, x in ((0, 0), (1, nx - 1)):
                if st == 3:
                    xs3[side, n] = f[n, side_rows(st, x), :]
                else:
                    xs[st, side, n] = f[n, side_rows(st, x), :]
        copies = halo_copies(st)
        for sends, _, copy in copies[2:] + copies[:2]:
            pl.when(sends)(copy.start)

    def take_halo(st):
        f = fields[st]
        for sends, receives, copy in halo_copies(st):
            pl.when(sends)(copy.wait_send)
            pl.when(receives)(copy.wait_recv)
        for n in range(f.shape[0]):
            for side, x in ((0, -1), (1, nx)):
                f[n, side_rows(st, x), :] = xr3[side, n] if st == 3 else xr[st, side, n]

    def deep_copies(kind):
        near = lambda ref, low, high: (ref.at[low:high] if len(ref.shape) == 2 else ref.at[:, low:high])
        if kind == 0:
            ups, downs = (cf, ny * nx, 0, nx), (cf, nx, (ny + 1) * nx, nx)
        elif kind == 1:
            ups = (fx, (ny + 1) * pitch - 8, pitch - 8, nx + 8)
            downs = (fx, 2 * pitch - 8, (ny + 2) * pitch - 8, nx + 8)
        elif kind == 2:
            ups, downs = (fy, ny * nx, 0, nx), (fy, 2 * nx, (ny + 2) * nx, nx)
        elif kind == 3:
            ups, downs = (f2, ny * pitch, 0, nx), (f2, 3 * pitch, (ny + 3) * pitch, nx)
        else:
            ups, downs = (coarse, cy, 0, 1), (coarse, 1, cy + 1, 1)
        return [
            (sends, receives, remote(near(ref, src, src + n), near(ref, dst, dst + n),
                                     w_send.at[kind, i], w_recv.at[kind, i], to))
            for i, (sends, receives, to, (ref, src, dst, n)) in enumerate((
                (up_y, down_y, (ix, iy + 1), ups), (down_y, up_y, (ix, iy - 1), downs)))
        ]

    def send_deep(*kinds):
        for kind in kinds:
            for sends, _, copy in deep_copies(kind):
                pl.when(sends)(copy.start)

    def take_deep(*kinds):
        for kind in kinds:
            for sends, receives, copy in deep_copies(kind):
                pl.when(sends)(copy.wait_send)
                pl.when(receives)(copy.wait_recv)

    def group_copies(kind, block, received):
        return [
            remote(block, received.at[d - 1], g_send.at[kind, d - 1], g_recv.at[kind, d - 1],
                   (ix, row * group + lax.rem(place + d, group)))
            for d in range(1, group)
        ]

    def row_copies(kind, block, received):
        return [
            (row + d < n_group, row >= d, remote(
                block, received.at[d - 1], g_send.at[kind, d - 1], g_recv.at[kind, d - 1],
                (ix, (row + d) * group + place)))
            for d in range(1, n_group)
        ]

    def plane(y):
        return Cells((y + 1) * nx, (y + 2) * pitch, nx)

    def inner(body, low=1, high=ny - 1, unroll=2):
        def step(y, _):
            body(Cells(pl.multiple_of((y + 1) * nx, 8), pl.multiple_of((y + 2) * pitch, 8), nx))
            return 0

        lax.fori_loop(low, high, step, 0, unroll=unroll)

    def columns(body, more=0):
        for x in (0, nx - 1):
            body(Cells((1 - more) * nx + x, (2 - more) * pitch + x, ny + 2 * more, nx, pitch))

    def outer(body):
        body(plane(0))
        body(plane(ny - 1))
        columns(body)

    def conductivity(u):
        t = f0[0, u.field(), :]
        f0[2, u.field(), :] = 1.0 + 4.0 * e_in[u.coef(), :] * (t * t * t)

    for load in loads:
        load.wait()
    inner(conductivity, 0, ny)
    n_halo = sum(v.astype(jnp.int32) for v in (up_y, down_y, up_x, down_x))
    pl.semaphore_wait(barrier, (group - 1) + (n_group - 1) + n_halo)
    send_halo(0)
    for load in more:
        load.wait()

    def block_sum(load, j, step):
        total = None
        for a in (0, step):
            for b in (0, 1):
                part = load(2 * j * step + a + b)
                total = part if total is None else total + part
        return total

    s_all = None
    for j in range(cy):
        cs = block_sum(lambda at: c_f[pl.ds(nx + at, cx, stride=2), :], j, nx)
        cond = block_sum(lambda at: f0[2, pl.ds(first_on + at, cx, stride=2), :], j, pitch)
        inv_solid = 1.0 / (4.0 * solid_cap + cs + lump_factor * cond)
        inv_denom = 1.0 / (4.0 * gas_cap + cs + 2.0 * flow_rate - cs * cs * inv_solid)
        slope = 2.0 * flow_rate * inv_denom
        coarse[CSUM, j + 1], coarse[ISOL, j + 1], coarse[SLOPE, j + 1] = cs, inv_solid, slope
        s_all = slope if s_all is None else s_all * slope
    s_blk[...] = s_all
    for copy in group_copies(0, s_blk, s_rec):
        copy.start()

    lane = lax.broadcasted_iota(jnp.int32, (1, nz), 1)
    not_last = (lane < nz - 1).astype(jnp.float32)
    not_first = (lane > 0).astype(jnp.float32)
    gas_zp = gas_conduct * 0.25 * not_last
    gas_zm = gas_conduct * 0.25 * not_first

    def set_up(u):
        c = f0[2, u.field(), :]
        xp = 0.5 * (c + f0[2, u.field(1), :])
        xm = 0.5 * (c + f0[2, u.field(-1), :])
        yp = 0.5 * (c + f0[2, u.field(pitch), :])
        ym = 0.5 * (c + f0[2, u.field(-pitch), :])
        zp = 0.125 * (c + not_last * pltpu.roll(c, nz - 1, 1))
        zm = 0.125 * (c + not_first * pltpu.roll(c, 1, 1))
        fx[u.field(), :] = xp
        if u.step is None:
            fx[pl.ds(u.on - 8, 8), :] = 0.5 * (f0[2, pl.ds(u.on - 8, 8), :] + f0[2, pl.ds(u.on - 7, 8), :])
        else:
            fx[u.field(-1), :] = xm
        fy[u.coef(), :] = ym
        fy[u.coef(nx), :] = yp
        cf[FZ, u.coef(), :] = not_last * zp
        k = c_f[u.coef(), :]
        sd = solid_cap + k + (((xp + xm) + (yp + ym)) + (zp + zm))
        gd = (gas_cap + flow_rate + gas_conduct * 2.0 * 2.25) + k
        w = relaxation / (sd * gd - k * k)
        diag[u.coef(), :] = sd
        cf[P_, u.coef(), :] = gd * w
        cf[Q_, u.coef(), :] = k * w
        cf[R_, u.coef(), :] = sd * w

    def beside(f, u):
        s = f[0, u.field(), :]
        g = f[1, u.field(), :]
        z = cf[FZ, u.coef(), :]
        hs = cf[B_S, u.coef(), :]
        hs += fy[u.coef(nx), :] * f[0, u.field(pitch), :]
        hs += fy[u.coef(), :] * f[0, u.field(-pitch), :]
        hs += fx[u.field(), :] * f[0, u.field(1), :]
        hs += fx[u.field(-1), :] * f[0, u.field(-1), :]
        hs += z * pltpu.roll(s, nz - 1, 1) + pltpu.roll(z * s, 1, 1)
        hg = cf[B_G, u.coef(), :]
        hg += (flow_rate + gas_conduct) * f[1, u.field(-pitch), :]
        hg += gas_conduct * (f[1, u.field(pitch), :] + (f[1, u.field(-1), :] + f[1, u.field(1), :]))
        hg += gas_zp * pltpu.roll(g, nz - 1, 1) + gas_zm * pltpu.roll(g, 1, 1)
        return s, g, hs, hg

    def relaxed(f, u):
        s, g, hs, hg = beside(f, u)
        p, q, r = (cf[n, u.coef(), :] for n in (P_, Q_, R_))
        keep = 1.0 - relaxation
        return keep * s + (p * hs + q * hg), keep * g + (q * hs + r * hg)

    def sweep(f, new):
        def body(u):
            new[0, u.field(), :], new[1, u.field(), :] = relaxed(f, u)

        return body

    inner(set_up)
    inner(sweep(f0, f1))
    take_halo(0)
    outer(set_up)
    outer(sweep(f0, f1))
    send_halo(1)
    send_deep(0, 1, 2)
    inner(sweep(f1, f2))

    def upstream(d):
        return jnp.full((cx, nz), place, jnp.int32) >= d

    for copy in group_copies(0, s_blk, s_rec):
        copy.wait()
    s_before = s_after = jnp.ones((cx, nz), jnp.float32)
    for d in range(1, group):
        s_d = s_rec[d - 1]
        s_before = jnp.where(upstream(d), s_before * s_d, s_before)
        s_after = jnp.where(upstream(d), s_after, s_after * s_d)
    s_pre[...] = s_before
    s_row[...] = s_before * s_blk[...] * s_after
    for sends, _, copy in row_copies(1, s_row, s_rrec):
        pl.when(sends)(copy.start)

    take_halo(1)
    outer(sweep(f1, f2))
    send_halo(2)
    send_deep(3)

    def residual(u):
        s, g, hs, hg = beside(f2, u)
        k = c_f[u.coef(), :]
        gd = (gas_cap + flow_rate + gas_conduct * 2.0 * 2.25) + k
        res[0, u.coef(), :] = hs - (diag[u.coef(), :] * s - k * g)
        res[1, u.coef(), :] = hg - (gd * g - k * s)

    inner(residual)
    take_halo(2)
    outer(residual)

    state = jnp.zeros((cx, nz), jnp.float32)
    for j in range(cy):
        r_s = block_sum(lambda at: res[0, pl.ds(nx + at, cx, stride=2), :], j, nx)
        r_g = block_sum(lambda at: res[1, pl.ds(nx + at, cx, stride=2), :], j, nx)
        slope = coarse[SLOPE, j + 1]
        offset = (r_g + coarse[CSUM, j + 1] * r_s * coarse[ISOL, j + 1]) * (slope * (0.5 / flow_rate))
        coarse[CRES, j + 1], coarse[OFFS, j + 1] = r_s, offset
        state = slope * state + offset
    o_blk[...] = state
    for copy in group_copies(2, o_blk, o_rec):
        copy.start()
    send_deep(4)
    for sends, receives, copy in row_copies(1, s_row, s_rrec):
        pl.when(sends)(copy.wait_send)
        pl.when(receives)(copy.wait_recv)
    for copy in group_copies(2, o_blk, o_rec):
        copy.wait()
    state = jnp.zeros((cx, nz), jnp.float32)
    for d in range(group - 1, 0, -1):
        state = jnp.where(upstream(d), s_rec[d - 1] * state + o_rec[d - 1], state)
    before = state
    state = s_blk[...] * state + o_blk[...]
    for d in range(group - 1, 0, -1):
        state = jnp.where(upstream(d), state, s_rec[d - 1] * state + o_rec[d - 1])
    o_row[...] = state
    for sends, _, copy in row_copies(3, o_row, o_rrec):
        pl.when(sends)(copy.start)
    for sends, receives, copy in row_copies(3, o_row, o_rrec):
        pl.when(sends)(copy.wait_send)
        pl.when(receives)(copy.wait_recv)
    state = jnp.zeros((cx, nz), jnp.float32)
    for d in range(n_group - 1, 0, -1):
        state = s_rrec[d - 1] * state + o_rrec[d - 1]
    error = s_pre[...] * state + before
    take_deep(0, 1, 2, 3, 4)
    for j in range(-1, cy + 1):
        if j >= 0:
            error = coarse[SLOPE, j + 1] * error + coarse[OFFS, j + 1]
        solid_error = (coarse[CRES, j + 1] + coarse[CSUM, j + 1] * error) * coarse[ISOL, j + 1]
        for y in (2 * j, 2 * j + 1):
            for b in (0, 1):
                at = pl.ds((y + 2) * pitch + b, cx, stride=2)
                f3[0, at, :] = f2[0, at, :] + solid_error
                f3[1, at, :] = f2[1, at, :] + error

    def last(u):
        o_v[0, u.coef(), :], o_v[1, u.coef(), :] = relaxed(f4, u)

    send_halo(3)
    inner(sweep(f3, f4), -1, ny + 1)
    take_halo(3)
    columns(sweep(f3, f4), 1)
    send_halo(4)
    inner(last, 0, ny)
    take_halo(4)
    columns(last)
    store = pltpu.make_async_copy(o_v.at[:, own], out, in_sem.at[0])
    store.start()
    store.wait()


def shards(n_gx, n_gy, temps, right_side, exchange, coupling):
    _, nx, ny, nz = temps.shape
    group = 8 if n_gy % 8 == 0 else 2
    n_group = n_gy // group
    rows, cx, cy = nx * ny, nx // 2, ny // 2
    f32 = jnp.float32
    padded = (nx + EDGE) * (ny + 4)
    ext = rows + 2 * nx
    kinds = max(group, n_group) - 1
    vmem = lambda *shape: pltpu.VMEM(shape, f32)
    line = lambda *lead: pltpu.VMEM((*lead, cx, nz), f32)
    scratch = [
        vmem(ext, nz), vmem(ext, nz), vmem(2, ext, nz),
        vmem(3, padded, nz), vmem(2, padded, nz), vmem(2, padded, nz), vmem(2, padded, nz), vmem(2, padded, nz),
        vmem(6, ext, nz), vmem(padded, nz), vmem(ext + nx, nz), vmem(ext, nz), vmem(2, ext, nz),
        vmem(STAGES, 2, 3, ny, nz), vmem(STAGES, 2, 3, ny, nz), vmem(2, 2, ny + 2, nz), vmem(2, 2, ny + 2, nz),
        line(5, cy + 2),
        line(), line(), line(group - 1), line(group - 1),
        line(), line(), line(n_group - 1), line(n_group - 1), line(),
        pltpu.SemaphoreType.DMA((3 + ny,)),
        pltpu.SemaphoreType.DMA((STAGES, 4)), pltpu.SemaphoreType.DMA((STAGES, 4)),
        pltpu.SemaphoreType.DMA((5, 2)), pltpu.SemaphoreType.DMA((5, 2)),
        pltpu.SemaphoreType.DMA((4, kinds)), pltpu.SemaphoreType.DMA((4, kinds)),
    ]
    flat = lambda a: jnp.swapaxes(a, -3, -2).reshape(*a.shape[:-3], rows, nz)
    out = pl.pallas_call(
        functools.partial(kernel, (nx, ny, nz, n_gx, n_gy, group)),
        out_shape=jax.ShapeDtypeStruct((2, rows, nz), f32),
        in_specs=[pl.BlockSpec(memory_space=pl.ANY)] * 4,
        out_specs=pl.BlockSpec(memory_space=pl.ANY),
        scratch_shapes=scratch,
        compiler_params=pltpu.CompilerParams(collective_id=0, has_side_effects=True),
    )(flat(temps), flat(right_side), flat(exchange), flat(coupling))
    return jnp.swapaxes(out.reshape(2, ny, nx, nz), 1, 2)


def solution(mesh):
    return jax.shard_map(
        functools.partial(shards, mesh.shape["gx"], mesh.shape["gy"]),
        mesh=mesh,
        in_specs=(
            P(None, "gx", "gy", None),
            P(None, "gx", "gy", None),
            P("gx", "gy", None),
            P("gx", "gy", None),
        ),
        out_specs=P(None, "gx", "gy", None),
        check_vma=False,
    )
```

```python
import functools

import jax
import jax.numpy as jnp
from jax import lax
from jax.experimental import pallas as pl
from jax.experimental.pallas import tpu as pltpu
from jax.sharding import PartitionSpec as P

MESH = pl.DeviceIdType.MESH
EDGE = 8

solid_cap = 0.5
gas_cap = 0.02
flow_rate = 40.0
gas_conduct = 0.05
relaxation = 0.8
lump_factor = 0.25
STAGES = 4


class Cells:
    def __init__(self, at, on, n, step=None, skip=None):
        self.at, self.on, self.n, self.step, self.skip = at, on, n, step, skip

    def coef(self, shift=0):
        return pl.ds(self.at + shift, self.n, stride=self.step)

    def field(self, shift=0):
        return pl.ds(self.on + shift, self.n, stride=self.skip)


def kernel(dims, temps, right, exch, coup, out, *scratch):
    nx, ny, nz, n_gx, n_gy, group = dims
    pitch = nx + EDGE
    cx, cy = nx // 2, ny // 2
    n_group = n_gy // group
    (e_in, c_f, o_v, f0, f1, f2, f3, f4, cf, fx, fy, diag, res, xs, xr, xs3, xr3, cs3, cr3, coarse,
     s_blk, o_blk, s_rec, o_rec, s_row, o_row, s_rrec, o_rrec, s_pre,
     in_sem, h_send, h_recv, w_send, w_recv, g_send, g_recv) = scratch
    P_, Q_, R_, FZ, B_S, B_G = range(6)
    CSUM, ISOL, CRES, SLOPE, OFFS = range(5)
    mine = slice(nx, (ny + 1) * nx)
    first_on = 2 * pitch
    ix, iy = lax.axis_index("gx"), lax.axis_index("gy")
    place, row = lax.rem(iy, group), lax.div(iy, group)

    loads = [
        pltpu.make_async_copy(temps.at[:, pl.ds(y * nx, nx)], f0.at[0:2, pl.ds((y + 2) * pitch, nx)], in_sem.at[3 + y])
        for y in range(ny)
    ]
    loads.append(pltpu.make_async_copy(exch, e_in.at[mine], in_sem.at[0]))
    more = [pltpu.make_async_copy(coup, c_f.at[mine], in_sem.at[1]), pltpu.make_async_copy(right, cf.at[B_S:B_G + 1, mine], in_sem.at[2])]
    for load in loads + more:
        load.start()

    barrier = pltpu.get_barrier_semaphore()

    def greet(gx, gy):
        pl.semaphore_signal(barrier, inc=1, device_id=(gx, gy), device_id_type=MESH)

    for d in range(1, group):
        greet(ix, row * group + lax.rem(place + d, group))
    for d in range(1, n_group):
        greet(ix, lax.rem(row + d, n_group) * group + place)
    up_y, down_y, up_x, down_x = iy < n_gy - 1, iy > 0, ix < n_gx - 1, ix > 0
    pl.when(up_y)(lambda: greet(ix, iy + 1))
    pl.when(down_y)(lambda: greet(ix, iy - 1))
    pl.when(up_x)(lambda: greet(ix + 1, iy))
    pl.when(down_x)(lambda: greet(ix - 1, iy))

    fields = (f0, f1, f2, f3, f4)
    plane_zero = jnp.zeros((nx, nz), jnp.float32)
    side_zero = jnp.zeros((ny, nz), jnp.float32)

    def clear_planes(y, far, face, line):
        for f in fields:
            for n in range(f.shape[0]):
                f[n, (y + 2) * pitch:(y + 2) * pitch + nx, :] = plane_zero
        for n in range(2):
            f2[n, (far + 2) * pitch:(far + 2) * pitch + nx, :] = plane_zero
        for n in range(6):
            cf[n, (y + 1) * nx:(y + 2) * nx, :] = plane_zero
        fx[(y + 2) * pitch - 8:(y + 2) * pitch + nx, :] = jnp.zeros((nx + 8, nz), jnp.float32)
        fy[face * nx:(face + 1) * nx, :] = plane_zero
        for n in range(5):
            coarse[n, line] = jnp.zeros((cx, nz), jnp.float32)

    def clear_sides(side):
        for st in range(STAGES):
            for n in range(3 if st == 0 else 2):
                xr[st, side, n] = side_zero
        for n in range(4):
            xr3[side, n] = jnp.zeros((ny + 2, nz), jnp.float32)
        for n in range(10):
            cr3[side, n] = side_zero

    pl.when(jnp.logical_not(down_y))(lambda: clear_planes(-1, -2, 0, 0))
    pl.when(jnp.logical_not(up_y))(lambda: clear_planes(ny, ny + 1, ny + 2, cy + 1))
    pl.when(jnp.logical_not(down_x))(lambda: clear_sides(0))
    pl.when(jnp.logical_not(up_x))(lambda: clear_sides(1))
    for d in range(1, n_group):

        @pl.when(row < d)
        def _():
            s_rrec[d - 1] = jnp.ones((cx, nz), jnp.float32)
            o_rrec[d - 1] = jnp.zeros((cx, nz), jnp.float32)

    def remote(src, dst, send, recv, to):
        return pltpu.make_async_remote_copy(
            src_ref=src, dst_ref=dst, send_sem=send, recv_sem=recv, device_id=to, device_id_type=MESH)

    def halo_copies(st):
        f = fields[st]
        nf = f.shape[0]
        plane = lambda y: f.at[:, (y + 2) * pitch:(y + 2) * pitch + nx]
        sides = (xs3, xr3) if st == 3 else (xs.at[st, :, :nf], xr.at[st, :, :nf])
        parts = [
            (up_x, down_x, sides[0].at[1], sides[1].at[0], (ix + 1, iy)),
            (down_x, up_x, sides[0].at[0], sides[1].at[1], (ix - 1, iy)),
        ]
        if st < 3:
            parts += [
                (up_y, down_y, plane(ny - 1), plane(-1), (ix, iy + 1)),
                (down_y, up_y, plane(0), plane(ny), (ix, iy - 1)),
            ]
        return [
            (sends, receives, remote(src, dst, h_send.at[st, i], h_recv.at[st, i], to))
            for i, (sends, receives, src, dst, to) in enumerate(parts)
        ]

    def side_rows(st, x):
        more = 1 if st == 3 else 0
        return pl.ds(first_on - more * pitch + x, ny + 2 * more, stride=pitch)

    def send_halo(st):
        f = fields[st]
        for n in range(f.shape[0]):
            for side, x, deeper in ((0, 0, 1), (1, nx - 1, nx - 2)):
                if st == 3:
                    xs3[side, n] = f[n, side_rows(st, x), :]
                    xs3[side, 2 + n] = f[n, side_rows(st, deeper), :]
                else:
                    xs[st, side, n] = f[n, side_rows(st, x), :]
        copies = halo_copies(st)
        for sends, _, copy in copies[2:] + copies[:2]:
            pl.when(sends)(copy.start)

    def take_halo(st):
        f = fields[st]
        for sends, receives, copy in halo_copies(st):
            pl.when(sends)(copy.wait_send)
            pl.when(receives)(copy.wait_recv)
        for n in range(f.shape[0]):
            for side, x, deeper in ((0, -1, -2), (1, nx, nx + 1)):
                if st == 3:
                    f[n, side_rows(st, x), :] = xr3[side, n]
                    f[n, side_rows(st, deeper), :] = xr3[side, 2 + n]
                else:
                    f[n, side_rows(st, x), :] = xr[st, side, n]

    def deep_copies(kind):
        if kind == 5:
            return [
                (up_x, down_x, remote(cs3.at[1], cr3.at[0], w_send.at[5, 0], w_recv.at[5, 0], (ix + 1, iy))),
                (down_x, up_x, remote(cs3.at[0], cr3.at[1], w_send.at[5, 1], w_recv.at[5, 1], (ix - 1, iy))),
            ]
        near = lambda ref, low, high: (ref.at[low:high] if len(ref.shape) == 2 else ref.at[:, low:high])
        if kind == 0:
            ups, downs = (cf, ny * nx, 0, nx), (cf, nx, (ny + 1) * nx, nx)
        elif kind == 1:
            ups = (fx, (ny + 1) * pitch - 8, pitch - 8, nx + 8)
            downs = (fx, 2 * pitch - 8, (ny + 2) * pitch - 8, nx + 8)
        elif kind == 2:
            ups, downs = (fy, ny * nx, 0, nx), (fy, 2 * nx, (ny + 2) * nx, nx)
        elif kind == 3:
            ups, downs = (f2, ny * pitch, 0, nx), (f2, 3 * pitch, (ny + 3) * pitch, nx)
        else:
            ups, downs = (coarse, cy, 0, 1), (coarse, 1, cy + 1, 1)
        return [
            (sends, receives, remote(near(ref, src, src + n), near(ref, dst, dst + n),
                                     w_send.at[kind, i], w_recv.at[kind, i], to))
            for i, (sends, receives, to, (ref, src, dst, n)) in enumerate((
                (up_y, down_y, (ix, iy + 1), ups), (down_y, up_y, (ix, iy - 1), downs)))
        ]

    def send_deep(*kinds):
        for kind in kinds:
            for sends, _, copy in deep_copies(kind):
                pl.when(sends)(copy.start)

    def take_deep(*kinds):
        for kind in kinds:
            for sends, receives, copy in deep_copies(kind):
                pl.when(sends)(copy.wait_send)
                pl.when(receives)(copy.wait_recv)

    def group_copies(kind, block, received):
        return [
            remote(block, received.at[d - 1], g_send.at[kind, d - 1], g_recv.at[kind, d - 1],
                   (ix, row * group + lax.rem(place + d, group)))
            for d in range(1, group)
        ]

    def row_copies(kind, block, received):
        return [
            (row + d < n_group, row >= d, remote(
                block, received.at[d - 1], g_send.at[kind, d - 1], g_recv.at[kind, d - 1],
                (ix, (row + d) * group + place)))
            for d in range(1, n_group)
        ]

    def plane(y):
        return Cells((y + 1) * nx, (y + 2) * pitch, nx)

    def inner(body, low=1, high=ny - 1, unroll=2):
        def step(y, _):
            body(Cells(pl.multiple_of((y + 1) * nx, 8), pl.multiple_of((y + 2) * pitch, 8), nx))
            return 0

        lax.fori_loop(low, high, step, 0, unroll=unroll)

    def columns(body, more=0, at=(0, nx - 1)):
        for x in at:
            body(Cells((1 - more) * nx + x, (2 - more) * pitch + x, ny + 2 * more, nx, pitch))

    def outer(body):
        body(plane(0))
        body(plane(ny - 1))
        columns(body)

    def conductivity(u):
        t = f0[0, u.field(), :]
        f0[2, u.field(), :] = 1.0 + 4.0 * e_in[u.coef(), :] * (t * t * t)

    for load in loads:
        load.wait()
    inner(conductivity, 0, ny)
    n_halo = sum(v.astype(jnp.int32) for v in (up_y, down_y, up_x, down_x))
    pl.semaphore_wait(barrier, (group - 1) + (n_group - 1) + n_halo)
    send_halo(0)
    for load in more:
        load.wait()

    def block_sum(load, j, step):
        total = None
        for a in (0, step):
            for b in (0, 1):
                part = load(2 * j * step + a + b)
                total = part if total is None else total + part
        return total

    s_all = None
    for j in range(cy):
        cs = block_sum(lambda at: c_f[pl.ds(nx + at, cx, stride=2), :], j, nx)
        cond = block_sum(lambda at: f0[2, pl.ds(first_on + at, cx, stride=2), :], j, pitch)
        inv_solid = 1.0 / (4.0 * solid_cap + cs + lump_factor * cond)
        inv_denom = 1.0 / (4.0 * gas_cap + cs + 2.0 * flow_rate - cs * cs * inv_solid)
        slope = 2.0 * flow_rate * inv_denom
        coarse[CSUM, j + 1], coarse[ISOL, j + 1], coarse[SLOPE, j + 1] = cs, inv_solid, slope
        s_all = slope if s_all is None else s_all * slope
    s_blk[...] = s_all
    for copy in group_copies(0, s_blk, s_rec):
        copy.start()

    lane = lax.broadcasted_iota(jnp.int32, (1, nz), 1)
    not_last = (lane < nz - 1).astype(jnp.float32)
    not_first = (lane > 0).astype(jnp.float32)
    gas_zp = gas_conduct * 0.25 * not_last
    gas_zm = gas_conduct * 0.25 * not_first

    def set_up(u):
        c = f0[2, u.field(), :]
        xp = 0.5 * (c + f0[2, u.field(1), :])
        xm = 0.5 * (c + f0[2, u.field(-1), :])
        yp = 0.5 * (c + f0[2, u.field(pitch), :])
        ym = 0.5 * (c + f0[2, u.field(-pitch), :])
        zp = 0.125 * (c + not_last * pltpu.roll(c, nz - 1, 1))
        zm = 0.125 * (c + not_first * pltpu.roll(c, 1, 1))
        fx[u.field(), :] = xp
        if u.step is None:
            fx[pl.ds(u.on - 8, 8), :] = 0.5 * (f0[2, pl.ds(u.on - 8, 8), :] + f0[2, pl.ds(u.on - 7, 8), :])
        else:
            fx[u.field(-1), :] = xm
        fy[u.coef(), :] = ym
        fy[u.coef(nx), :] = yp
        cf[FZ, u.coef(), :] = not_last * zp
        k = c_f[u.coef(), :]
        sd = solid_cap + k + (((xp + xm) + (yp + ym)) + (zp + zm))
        gd = (gas_cap + flow_rate + gas_conduct * 2.0 * 2.25) + k
        w = relaxation / (sd * gd - k * k)
        diag[u.coef(), :] = sd
        cf[P_, u.coef(), :] = gd * w
        cf[Q_, u.coef(), :] = k * w
        cf[R_, u.coef(), :] = sd * w

    class Given:
        def __init__(self, x, side):
            self.on, self.side = first_on + x, side

        def field(self, shift=0):
            return pl.ds(self.on + shift, ny, stride=pitch)

        def own(self, n):
            return cr3[self.side, n]

        def faces(self):
            return tuple(cr3[self.side, n] for n in (6, 7, 8, 9))

    def own(u, n):
        return u.own(n) if isinstance(u, Given) else cf[n, u.coef(), :]

    def faces(u):
        if isinstance(u, Given):
            return u.faces()
        return fx[u.field(-1), :], fx[u.field(), :], fy[u.coef(), :], fy[u.coef(nx), :]

    def beside(f, u):
        s = f[0, u.field(), :]
        g = f[1, u.field(), :]
        z = own(u, FZ)
        xm, xp, ym, yp = faces(u)
        hs = own(u, B_S)
        hs += yp * f[0, u.field(pitch), :]
        hs += ym * f[0, u.field(-pitch), :]
        hs += xp * f[0, u.field(1), :]
        hs += xm * f[0, u.field(-1), :]
        hs += z * pltpu.roll(s, nz - 1, 1) + pltpu.roll(z * s, 1, 1)
        hg = own(u, B_G)
        hg += (flow_rate + gas_conduct) * f[1, u.field(-pitch), :]
        hg += gas_conduct * (f[1, u.field(pitch), :] + (f[1, u.field(-1), :] + f[1, u.field(1), :]))
        hg += gas_zp * pltpu.roll(g, nz - 1, 1) + gas_zm * pltpu.roll(g, 1, 1)
        return s, g, hs, hg

    def relaxed(f, u):
        s, g, hs, hg = beside(f, u)
        p, q, r = own(u, P_), own(u, Q_), own(u, R_)
        keep = 1.0 - relaxation
        return keep * s + (p * hs + q * hg), keep * g + (q * hs + r * hg)

    def sweep(f, new):
        def body(u):
            new[0, u.field(), :], new[1, u.field(), :] = relaxed(f, u)

        return body

    inner(set_up)
    inner(sweep(f0, f1))
    take_halo(0)
    outer(set_up)
    outer(sweep(f0, f1))
    send_halo(1)
    for side, x in ((0, 0), (1, nx - 1)):
        u = Cells(nx + x, first_on + x, ny, nx, pitch)
        for n in range(6):
            cs3[side, n] = cf[n, u.coef(), :]
        cs3[side, 6], cs3[side, 7] = fx[u.field(-1), :], fx[u.field(), :]
        cs3[side, 8], cs3[side, 9] = fy[u.coef(), :], fy[u.coef(nx), :]
    send_deep(0, 1, 2, 5)
    inner(sweep(f1, f2))

    def upstream(d):
        return jnp.full((cx, nz), place, jnp.int32) >= d

    for copy in group_copies(0, s_blk, s_rec):
        copy.wait()
    s_before = s_after = jnp.ones((cx, nz), jnp.float32)
    for d in range(1, group):
        s_d = s_rec[d - 1]
        s_before = jnp.where(upstream(d), s_before * s_d, s_before)
        s_after = jnp.where(upstream(d), s_after, s_after * s_d)
    s_pre[...] = s_before
    s_row[...] = s_before * s_blk[...] * s_after
    for sends, _, copy in row_copies(1, s_row, s_rrec):
        pl.when(sends)(copy.start)

    take_halo(1)
    outer(sweep(f1, f2))
    send_halo(2)
    send_deep(3)

    def residual(u):
        s, g, hs, hg = beside(f2, u)
        k = c_f[u.coef(), :]
        gd = (gas_cap + flow_rate + gas_conduct * 2.0 * 2.25) + k
        res[0, u.coef(), :] = hs - (diag[u.coef(), :] * s - k * g)
        res[1, u.coef(), :] = hg - (gd * g - k * s)

    inner(residual)
    take_halo(2)
    outer(residual)

    state = jnp.zeros((cx, nz), jnp.float32)
    for j in range(cy):
        r_s = block_sum(lambda at: res[0, pl.ds(nx + at, cx, stride=2), :], j, nx)
        r_g = block_sum(lambda at: res[1, pl.ds(nx + at, cx, stride=2), :], j, nx)
        slope = coarse[SLOPE, j + 1]
        offset = (r_g + coarse[CSUM, j + 1] * r_s * coarse[ISOL, j + 1]) * (slope * (0.5 / flow_rate))
        coarse[CRES, j + 1], coarse[OFFS, j + 1] = r_s, offset
        state = slope * state + offset
    o_blk[...] = state
    for copy in group_copies(2, o_blk, o_rec):
        copy.start()
    send_deep(4)
    for sends, receives, copy in row_copies(1, s_row, s_rrec):
        pl.when(sends)(copy.wait_send)
        pl.when(receives)(copy.wait_recv)
    for copy in group_copies(2, o_blk, o_rec):
        copy.wait()
    state = jnp.zeros((cx, nz), jnp.float32)
    for d in range(group - 1, 0, -1):
        state = jnp.where(upstream(d), s_rec[d - 1] * state + o_rec[d - 1], state)
    before = state
    state = s_blk[...] * state + o_blk[...]
    for d in range(group - 1, 0, -1):
        state = jnp.where(upstream(d), state, s_rec[d - 1] * state + o_rec[d - 1])
    o_row[...] = state
    for sends, _, copy in row_copies(3, o_row, o_rrec):
        pl.when(sends)(copy.start)
    for sends, receives, copy in row_copies(3, o_row, o_rrec):
        pl.when(sends)(copy.wait_send)
        pl.when(receives)(copy.wait_recv)
    state = jnp.zeros((cx, nz), jnp.float32)
    for d in range(n_group - 1, 0, -1):
        state = s_rrec[d - 1] * state + o_rrec[d - 1]
    error = s_pre[...] * state + before
    take_deep(0, 1, 2, 3, 4, 5)
    for j in range(-1, cy + 1):
        if j >= 0:
            error = coarse[SLOPE, j + 1] * error + coarse[OFFS, j + 1]
        solid_error = (coarse[CRES, j + 1] + coarse[CSUM, j + 1] * error) * coarse[ISOL, j + 1]
        for y in (2 * j, 2 * j + 1):
            for b in (0, 1):
                at = pl.ds((y + 2) * pitch + b, cx, stride=2)
                f3[0, at, :] = f2[0, at, :] + solid_error
                f3[1, at, :] = f2[1, at, :] + error

    def last(u):
        o_v[0, u.coef(), :], o_v[1, u.coef(), :] = relaxed(f4, u)

    send_halo(3)
    inner(sweep(f3, f4), -1, ny + 1)
    inner(last, 0, ny)
    take_halo(3)
    columns(sweep(f3, f4), 1)
    sweep(f3, f4)(Given(-1, 0))
    sweep(f3, f4)(Given(nx, 1))
    columns(last, 0, (0, 1, nx - 2, nx - 1))
    store = pltpu.make_async_copy(o_v.at[:, mine], out, in_sem.at[0])
    store.start()
    store.wait()


def shards(n_gx, n_gy, temps, right_side, exchange, coupling):
    _, nx, ny, nz = temps.shape
    group = 8 if n_gy % 8 == 0 else 2
    n_group = n_gy // group
    rows, cx, cy = nx * ny, nx // 2, ny // 2
    f32 = jnp.float32
    padded = (nx + EDGE) * (ny + 4)
    ext = rows + 2 * nx
    kinds = max(group, n_group) - 1
    vmem = lambda *shape: pltpu.VMEM(shape, f32)
    line = lambda *lead: pltpu.VMEM((*lead, cx, nz), f32)
    scratch = [
        vmem(ext, nz), vmem(ext, nz), vmem(2, ext, nz),
        vmem(3, padded, nz), vmem(2, padded, nz), vmem(2, padded, nz), vmem(2, padded, nz), vmem(2, padded, nz),
        vmem(6, ext, nz), vmem(padded, nz), vmem(ext + nx, nz), vmem(ext, nz), vmem(2, ext, nz),
        vmem(STAGES, 2, 3, ny, nz), vmem(STAGES, 2, 3, ny, nz), vmem(2, 4, ny + 2, nz), vmem(2, 4, ny + 2, nz), vmem(2, 10, ny, nz), vmem(2, 10, ny, nz),
        line(5, cy + 2),
        line(), line(), line(group - 1), line(group - 1),
        line(), line(), line(n_group - 1), line(n_group - 1), line(),
        pltpu.SemaphoreType.DMA((3 + ny,)),
        pltpu.SemaphoreType.DMA((STAGES, 4)), pltpu.SemaphoreType.DMA((STAGES, 4)),
        pltpu.SemaphoreType.DMA((6, 2)), pltpu.SemaphoreType.DMA((6, 2)),
        pltpu.SemaphoreType.DMA((4, kinds)), pltpu.SemaphoreType.DMA((4, kinds)),
    ]
    flat = lambda a: jnp.swapaxes(a, -3, -2).reshape(*a.shape[:-3], rows, nz)
    out = pl.pallas_call(
        functools.partial(kernel, (nx, ny, nz, n_gx, n_gy, group)),
        out_shape=jax.ShapeDtypeStruct((2, rows, nz), f32),
        in_specs=[pl.BlockSpec(memory_space=pl.ANY)] * 4,
        out_specs=pl.BlockSpec(memory_space=pl.ANY),
        scratch_shapes=scratch,
        compiler_params=pltpu.CompilerParams(collective_id=0, has_side_effects=True),
    )(flat(temps), flat(right_side), flat(exchange), flat(coupling))
    return jnp.swapaxes(out.reshape(2, ny, nx, nz), 1, 2)


def solution(mesh):
    return jax.shard_map(
        functools.partial(shards, mesh.shape["gx"], mesh.shape["gy"]),
        mesh=mesh,
        in_specs=(
            P(None, "gx", "gy", None),
            P(None, "gx", "gy", None),
            P("gx", "gy", None),
            P("gx", "gy", None),
        ),
        out_specs=P(None, "gx", "gy", None),
        check_vma=False,
    )
```

```python
import functools

import jax
import jax.numpy as jnp
from jax import lax
from jax.experimental import pallas as pl
from jax.experimental.pallas import tpu as pltpu
from jax.sharding import PartitionSpec as P

MESH = pl.DeviceIdType.MESH
EDGE = 8

solid_cap = 0.5
gas_cap = 0.02
flow_rate = 40.0
gas_conduct = 0.05
relaxation = 0.8
lump_factor = 0.25
STAGES = 4
REACH = 2


class Cells:
    def __init__(self, at, on, n, step=None, skip=None):
        self.at, self.on, self.n, self.step, self.skip = at, on, n, step, skip

    def coef(self, shift=0):
        return pl.ds(self.at + shift, self.n, stride=self.step)

    def field(self, shift=0):
        return pl.ds(self.on + shift, self.n, stride=self.skip)


def kernel(dims, temps, right, exch, coup, out, *scratch):
    nx, ny, nz, n_gx, n_gy, group = dims
    pitch = nx + EDGE
    cx, cy = nx // 2, ny // 2
    n_group = n_gy // group
    (e_in, c_f, o_v, f0, f1, f2, f3, f4, cf, fx, fy, diag, res, xs, xr, xs3, xr3, cs3, cr3, coarse,
     s_blk, o_blk, s_rec, o_rec, s_row, o_row, s_rrec, o_rrec, s_pre,
     news, in_sem, h_send, h_recv, w_send, w_recv, g_send, g_recv) = scratch
    P_, Q_, R_, FZ, B_S, B_G = range(6)
    CSUM, ISOL, CRES, SLOPE, OFFS = range(5)
    mine = slice(nx, (ny + 1) * nx)
    first_on = 2 * pitch
    ix, iy = lax.axis_index("gx"), lax.axis_index("gy")
    place, row = lax.rem(iy, group), lax.div(iy, group)

    loads = [
        pltpu.make_async_copy(temps.at[:, pl.ds(y * nx, nx)], f0.at[0:2, pl.ds((y + 2) * pitch, nx)], in_sem.at[3 + y])
        for y in range(ny)
    ]
    loads.append(pltpu.make_async_copy(exch, e_in.at[mine], in_sem.at[0]))
    more = [pltpu.make_async_copy(coup, c_f.at[mine], in_sem.at[1]), pltpu.make_async_copy(right, cf.at[B_S:B_G + 1, mine], in_sem.at[2])]
    for load in loads + more:
        load.start()

    barrier = pltpu.get_barrier_semaphore()

    def greet(gx, gy):
        pl.semaphore_signal(barrier, inc=1, device_id=(gx, gy), device_id_type=MESH)

    for d in range(1, group):
        greet(ix, row * group + lax.rem(place + d, group))
    near_rows = [(row + d < n_group, row + d) for d in range(1, min(REACH, n_group - 1) + 1)]
    near_rows += [(row >= d, row - d) for d in range(1, min(REACH, n_group - 1) + 1)]
    for there, other in near_rows:
        pl.when(there)(lambda other=other: greet(ix, other * group + place))
    up_y, down_y, up_x, down_x = iy < n_gy - 1, iy > 0, ix < n_gx - 1, ix > 0
    pl.when(up_y)(lambda: greet(ix, iy + 1))
    pl.when(down_y)(lambda: greet(ix, iy - 1))
    pl.when(up_x)(lambda: greet(ix + 1, iy))
    pl.when(down_x)(lambda: greet(ix - 1, iy))

    fields = (f0, f1, f2, f3, f4)
    plane_zero = jnp.zeros((nx, nz), jnp.float32)
    side_zero = jnp.zeros((ny, nz), jnp.float32)

    def clear_planes(y, far, face, line):
        for f in fields:
            for n in range(f.shape[0]):
                f[n, (y + 2) * pitch:(y + 2) * pitch + nx, :] = plane_zero
        for n in range(2):
            f2[n, (far + 2) * pitch:(far + 2) * pitch + nx, :] = plane_zero
        for n in range(6):
            cf[n, (y + 1) * nx:(y + 2) * nx, :] = plane_zero
        fx[(y + 2) * pitch - 8:(y + 2) * pitch + nx, :] = jnp.zeros((nx + 8, nz), jnp.float32)
        fy[face * nx:(face + 1) * nx, :] = plane_zero
        for n in range(5):
            coarse[n, line] = jnp.zeros((cx, nz), jnp.float32)

    def clear_sides(side):
        for st in range(STAGES):
            for n in range(3 if st == 0 else 2):
                xr[st, side, n] = side_zero
        for n in range(4):
            xr3[side, n] = jnp.zeros((ny + 2, nz), jnp.float32)
        for n in range(10):
            cr3[side, n] = side_zero

    pl.when(jnp.logical_not(down_y))(lambda: clear_planes(-1, -2, 0, 0))
    pl.when(jnp.logical_not(up_y))(lambda: clear_planes(ny, ny + 1, ny + 2, cy + 1))
    pl.when(jnp.logical_not(down_x))(lambda: clear_sides(0))
    pl.when(jnp.logical_not(up_x))(lambda: clear_sides(1))
    for d in range(1, n_group):

        @pl.when(row < d)
        def _():
            s_rrec[d - 1] = jnp.ones((cx, nz), jnp.float32)
            o_rrec[d - 1] = jnp.zeros((cx, nz), jnp.float32)

    def remote(src, dst, send, recv, to):
        return pltpu.make_async_remote_copy(
            src_ref=src, dst_ref=dst, send_sem=send, recv_sem=recv, device_id=to, device_id_type=MESH)

    def halo_copies(st):
        f = fields[st]
        nf = f.shape[0]
        plane = lambda y: f.at[:, (y + 2) * pitch:(y + 2) * pitch + nx]
        sides = (xs3, xr3) if st == 3 else (xs.at[st, :, :nf], xr.at[st, :, :nf])
        parts = [
            (up_x, down_x, sides[0].at[1], sides[1].at[0], (ix + 1, iy)),
            (down_x, up_x, sides[0].at[0], sides[1].at[1], (ix - 1, iy)),
        ]
        if st < 3:
            parts += [
                (up_y, down_y, plane(ny - 1), plane(-1), (ix, iy + 1)),
                (down_y, up_y, plane(0), plane(ny), (ix, iy - 1)),
            ]
        return [
            (sends, receives, remote(src, dst, h_send.at[st, i], h_recv.at[st, i], to))
            for i, (sends, receives, src, dst, to) in enumerate(parts)
        ]

    def side_rows(st, x):
        more = 1 if st == 3 else 0
        return pl.ds(first_on - more * pitch + x, ny + 2 * more, stride=pitch)

    def send_halo(st):
        f = fields[st]
        for n in range(f.shape[0]):
            for side, x, deeper in ((0, 0, 1), (1, nx - 1, nx - 2)):
                if st == 3:
                    xs3[side, n] = f[n, side_rows(st, x), :]
                    xs3[side, 2 + n] = f[n, side_rows(st, deeper), :]
                else:
                    xs[st, side, n] = f[n, side_rows(st, x), :]
        copies = halo_copies(st)
        for sends, _, copy in copies[2:] + copies[:2]:
            pl.when(sends)(copy.start)

    def take_halo(st):
        f = fields[st]
        for sends, receives, copy in halo_copies(st):
            pl.when(sends)(copy.wait_send)
            pl.when(receives)(copy.wait_recv)
        for n in range(f.shape[0]):
            for side, x, deeper in ((0, -1, -2), (1, nx, nx + 1)):
                if st == 3:
                    f[n, side_rows(st, x), :] = xr3[side, n]
                    f[n, side_rows(st, deeper), :] = xr3[side, 2 + n]
                else:
                    f[n, side_rows(st, x), :] = xr[st, side, n]

    def deep_copies(kind):
        if kind == 5:
            return [
                (up_x, down_x, remote(cs3.at[1], cr3.at[0], w_send.at[5, 0], w_recv.at[5, 0], (ix + 1, iy))),
                (down_x, up_x, remote(cs3.at[0], cr3.at[1], w_send.at[5, 1], w_recv.at[5, 1], (ix - 1, iy))),
            ]
        near = lambda ref, low, high: (ref.at[low:high] if len(ref.shape) == 2 else ref.at[:, low:high])
        if kind == 0:
            ups, downs = (cf, ny * nx, 0, nx), (cf, nx, (ny + 1) * nx, nx)
        elif kind == 1:
            ups = (fx, (ny + 1) * pitch - 8, pitch - 8, nx + 8)
            downs = (fx, 2 * pitch - 8, (ny + 2) * pitch - 8, nx + 8)
        elif kind == 2:
            ups, downs = (fy, ny * nx, 0, nx), (fy, 2 * nx, (ny + 2) * nx, nx)
        elif kind == 3:
            ups, downs = (f2, ny * pitch, 0, nx), (f2, 3 * pitch, (ny + 3) * pitch, nx)
        else:
            ups, downs = (coarse, cy, 0, 1), (coarse, 1, cy + 1, 1)
        return [
            (sends, receives, remote(near(ref, src, src + n), near(ref, dst, dst + n),
                                     w_send.at[kind, i], w_recv.at[kind, i], to))
            for i, (sends, receives, to, (ref, src, dst, n)) in enumerate((
                (up_y, down_y, (ix, iy + 1), ups), (down_y, up_y, (ix, iy - 1), downs)))
        ]

    def send_deep(*kinds):
        for kind in kinds:
            for sends, _, copy in deep_copies(kind):
                pl.when(sends)(copy.start)

    def take_deep(*kinds):
        for kind in kinds:
            for sends, receives, copy in deep_copies(kind):
                pl.when(sends)(copy.wait_send)
                pl.when(receives)(copy.wait_recv)

    def group_copies(kind, block, received):
        return [
            remote(block, received.at[d - 1], g_send.at[kind, d - 1], g_recv.at[kind, d - 1],
                   (ix, row * group + lax.rem(place + d, group)))
            for d in range(1, group)
        ]

    def row_copies(kind, block, received):
        return [
            (row + d < n_group, row >= d, remote(
                block, received.at[d - 1], g_send.at[kind, d - 1], g_recv.at[kind, d - 1],
                (ix, (row + d) * group + place)))
            for d in range(1, n_group)
        ]

    def plane(y):
        return Cells((y + 1) * nx, (y + 2) * pitch, nx)

    def inner(body, low=1, high=ny - 1, unroll=2):
        def step(y, _):
            body(Cells(pl.multiple_of((y + 1) * nx, 8), pl.multiple_of((y + 2) * pitch, 8), nx))
            return 0

        lax.fori_loop(low, high, step, 0, unroll=unroll)

    def columns(body, more=0, at=(0, nx - 1)):
        for x in at:
            body(Cells((1 - more) * nx + x, (2 - more) * pitch + x, ny + 2 * more, nx, pitch))

    def outer(body):
        body(plane(0))
        body(plane(ny - 1))
        columns(body)

    def conductivity(u):
        t = f0[0, u.field(), :]
        f0[2, u.field(), :] = 1.0 + 4.0 * e_in[u.coef(), :] * (t * t * t)

    for load in loads:
        load.wait()
    inner(conductivity, 0, ny)
    n_some = sum(v.astype(jnp.int32) for v in (up_y, down_y, up_x, down_x, *(there for there, _ in near_rows)))
    pl.semaphore_wait(barrier, group - 1 + n_some)
    send_halo(0)

    rounds = max(0, -(-(n_group - 1 - REACH) // REACH))

    def tell(k):
        if k < rounds:

            @pl.when(row >= REACH)
            def _():
                pl.semaphore_signal(
                    news.at[k], inc=1, device_id=(ix, (row - REACH) * group + place), device_id_type=MESH)

    def hear(k):
        if k < rounds:
            pl.when(row + REACH < n_group)(lambda: pl.semaphore_wait(news.at[k], 1))

    tell(0)
    for load in more:
        load.wait()

    def block_sum(load, j, step):
        total = None
        for a in (0, step):
            for b in (0, 1):
                part = load(2 * j * step + a + b)
                total = part if total is None else total + part
        return total

    s_all = None
    for j in range(cy):
        cs = block_sum(lambda at: c_f[pl.ds(nx + at, cx, stride=2), :], j, nx)
        cond = block_sum(lambda at: f0[2, pl.ds(first_on + at, cx, stride=2), :], j, pitch)
        inv_solid = 1.0 / (4.0 * solid_cap + cs + lump_factor * cond)
        inv_denom = 1.0 / (4.0 * gas_cap + cs + 2.0 * flow_rate - cs * cs * inv_solid)
        slope = 2.0 * flow_rate * inv_denom
        coarse[CSUM, j + 1], coarse[ISOL, j + 1], coarse[SLOPE, j + 1] = cs, inv_solid, slope
        s_all = slope if s_all is None else s_all * slope
    s_blk[...] = s_all
    for copy in group_copies(0, s_blk, s_rec):
        copy.start()

    lane = lax.broadcasted_iota(jnp.int32, (1, nz), 1)
    not_last = (lane < nz - 1).astype(jnp.float32)
    not_first = (lane > 0).astype(jnp.float32)
    gas_zp = gas_conduct * 0.25 * not_last
    gas_zm = gas_conduct * 0.25 * not_first

    def set_up(u):
        c = f0[2, u.field(), :]
        xp = 0.5 * (c + f0[2, u.field(1), :])
        xm = 0.5 * (c + f0[2, u.field(-1), :])
        yp = 0.5 * (c + f0[2, u.field(pitch), :])
        ym = 0.5 * (c + f0[2, u.field(-pitch), :])
        zp = 0.125 * (c + not_last * pltpu.roll(c, nz - 1, 1))
        zm = 0.125 * (c + not_first * pltpu.roll(c, 1, 1))
        fx[u.field(), :] = xp
        if u.step is None:
            fx[pl.ds(u.on - 8, 8), :] = 0.5 * (f0[2, pl.ds(u.on - 8, 8), :] + f0[2, pl.ds(u.on - 7, 8), :])
        else:
            fx[u.field(-1), :] = xm
        fy[u.coef(), :] = ym
        fy[u.coef(nx), :] = yp
        cf[FZ, u.coef(), :] = not_last * zp
        k = c_f[u.coef(), :]
        sd = solid_cap + k + (((xp + xm) + (yp + ym)) + (zp + zm))
        gd = (gas_cap + flow_rate + gas_conduct * 2.0 * 2.25) + k
        w = relaxation / (sd * gd - k * k)
        diag[u.coef(), :] = sd
        cf[P_, u.coef(), :] = gd * w
        cf[Q_, u.coef(), :] = k * w
        cf[R_, u.coef(), :] = sd * w

    class Given:
        def __init__(self, x, side):
            self.on, self.side = first_on + x, side

        def field(self, shift=0):
            return pl.ds(self.on + shift, ny, stride=pitch)

        def own(self, n):
            return cr3[self.side, n]

        def faces(self):
            return tuple(cr3[self.side, n] for n in (6, 7, 8, 9))

    def own(u, n):
        return u.own(n) if isinstance(u, Given) else cf[n, u.coef(), :]

    def faces(u):
        if isinstance(u, Given):
            return u.faces()
        return fx[u.field(-1), :], fx[u.field(), :], fy[u.coef(), :], fy[u.coef(nx), :]

    def beside(f, u):
        s = f[0, u.field(), :]
        g = f[1, u.field(), :]
        z = own(u, FZ)
        xm, xp, ym, yp = faces(u)
        hs = own(u, B_S)
        hs += yp * f[0, u.field(pitch), :]
        hs += ym * f[0, u.field(-pitch), :]
        hs += xp * f[0, u.field(1), :]
        hs += xm * f[0, u.field(-1), :]
        hs += z * pltpu.roll(s, nz - 1, 1) + pltpu.roll(z * s, 1, 1)
        hg = own(u, B_G)
        hg += (flow_rate + gas_conduct) * f[1, u.field(-pitch), :]
        hg += gas_conduct * (f[1, u.field(pitch), :] + (f[1, u.field(-1), :] + f[1, u.field(1), :]))
        hg += gas_zp * pltpu.roll(g, nz - 1, 1) + gas_zm * pltpu.roll(g, 1, 1)
        return s, g, hs, hg

    def relaxed(f, u):
        s, g, hs, hg = beside(f, u)
        p, q, r = own(u, P_), own(u, Q_), own(u, R_)
        keep = 1.0 - relaxation
        return keep * s + (p * hs + q * hg), keep * g + (q * hs + r * hg)

    def sweep(f, new):
        def body(u):
            new[0, u.field(), :], new[1, u.field(), :] = relaxed(f, u)

        return body

    inner(set_up)
    inner(sweep(f0, f1))
    hear(0)
    tell(1)
    take_halo(0)
    outer(set_up)
    outer(sweep(f0, f1))
    send_halo(1)
    for side, x in ((0, 0), (1, nx - 1)):
        u = Cells(nx + x, first_on + x, ny, nx, pitch)
        for n in range(6):
            cs3[side, n] = cf[n, u.coef(), :]
        cs3[side, 6], cs3[side, 7] = fx[u.field(-1), :], fx[u.field(), :]
        cs3[side, 8], cs3[side, 9] = fy[u.coef(), :], fy[u.coef(nx), :]
    send_deep(0, 1, 2, 5)
    inner(sweep(f1, f2))

    def upstream(d):
        return jnp.full((cx, nz), place, jnp.int32) >= d

    for copy in group_copies(0, s_blk, s_rec):
        copy.wait()
    s_before = s_after = jnp.ones((cx, nz), jnp.float32)
    for d in range(1, group):
        s_d = s_rec[d - 1]
        s_before = jnp.where(upstream(d), s_before * s_d, s_before)
        s_after = jnp.where(upstream(d), s_after, s_after * s_d)
    s_pre[...] = s_before
    s_row[...] = s_before * s_blk[...] * s_after
    hear(1)
    tell(2)

    take_halo(1)
    outer(sweep(f1, f2))
    send_halo(2)
    send_deep(3)

    def residual(u):
        s, g, hs, hg = beside(f2, u)
        k = c_f[u.coef(), :]
        gd = (gas_cap + flow_rate + gas_conduct * 2.0 * 2.25) + k
        res[0, u.coef(), :] = hs - (diag[u.coef(), :] * s - k * g)
        res[1, u.coef(), :] = hg - (gd * g - k * s)

    inner(residual)
    for k in range(2, rounds):
        hear(k)
        tell(k + 1)
    for sends, _, copy in row_copies(1, s_row, s_rrec):
        pl.when(sends)(copy.start)
    take_halo(2)
    outer(residual)

    state = jnp.zeros((cx, nz), jnp.float32)
    for j in range(cy):
        r_s = block_sum(lambda at: res[0, pl.ds(nx + at, cx, stride=2), :], j, nx)
        r_g = block_sum(lambda at: res[1, pl.ds(nx + at, cx, stride=2), :], j, nx)
        slope = coarse[SLOPE, j + 1]
        offset = (r_g + coarse[CSUM, j + 1] * r_s * coarse[ISOL, j + 1]) * (slope * (0.5 / flow_rate))
        coarse[CRES, j + 1], coarse[OFFS, j + 1] = r_s, offset
        state = slope * state + offset
    o_blk[...] = state
    for copy in group_copies(2, o_blk, o_rec):
        copy.start()
    send_deep(4)
    for sends, receives, copy in row_copies(1, s_row, s_rrec):
        pl.when(sends)(copy.wait_send)
        pl.when(receives)(copy.wait_recv)
    for copy in group_copies(2, o_blk, o_rec):
        copy.wait()
    state = jnp.zeros((cx, nz), jnp.float32)
    for d in range(group - 1, 0, -1):
        state = jnp.where(upstream(d), s_rec[d - 1] * state + o_rec[d - 1], state)
    before = state
    state = s_blk[...] * state + o_blk[...]
    for d in range(group - 1, 0, -1):
        state = jnp.where(upstream(d), state, s_rec[d - 1] * state + o_rec[d - 1])
    o_row[...] = state
    for sends, _, copy in row_copies(3, o_row, o_rrec):
        pl.when(sends)(copy.start)
    for sends, receives, copy in row_copies(3, o_row, o_rrec):
        pl.when(sends)(copy.wait_send)
        pl.when(receives)(copy.wait_recv)
    state = jnp.zeros((cx, nz), jnp.float32)
    for d in range(n_group - 1, 0, -1):
        state = s_rrec[d - 1] * state + o_rrec[d - 1]
    error = s_pre[...] * state + before
    take_deep(0, 1, 2, 3, 4, 5)
    for j in range(-1, cy + 1):
        if j >= 0:
            error = coarse[SLOPE, j + 1] * error + coarse[OFFS, j + 1]
        solid_error = (coarse[CRES, j + 1] + coarse[CSUM, j + 1] * error) * coarse[ISOL, j + 1]
        for y in (2 * j, 2 * j + 1):
            for b in (0, 1):
                at = pl.ds((y + 2) * pitch + b, cx, stride=2)
                f3[0, at, :] = f2[0, at, :] + solid_error
                f3[1, at, :] = f2[1, at, :] + error

    def last(u):
        o_v[0, u.coef(), :], o_v[1, u.coef(), :] = relaxed(f4, u)

    send_halo(3)
    inner(sweep(f3, f4), -1, ny + 1)
    inner(last, 0, ny)
    take_halo(3)
    columns(sweep(f3, f4), 1)
    sweep(f3, f4)(Given(-1, 0))
    sweep(f3, f4)(Given(nx, 1))
    columns(last, 0, (0, 1, nx - 2, nx - 1))
    store = pltpu.make_async_copy(o_v.at[:, mine], out, in_sem.at[0])
    store.start()
    store.wait()


def shards(n_gx, n_gy, temps, right_side, exchange, coupling):
    _, nx, ny, nz = temps.shape
    group = 8 if n_gy % 8 == 0 else 2
    n_group = n_gy // group
    rows, cx, cy = nx * ny, nx // 2, ny // 2
    f32 = jnp.float32
    padded = (nx + EDGE) * (ny + 4)
    ext = rows + 2 * nx
    kinds = max(group, n_group) - 1
    vmem = lambda *shape: pltpu.VMEM(shape, f32)
    line = lambda *lead: pltpu.VMEM((*lead, cx, nz), f32)
    scratch = [
        vmem(ext, nz), vmem(ext, nz), vmem(2, ext, nz),
        vmem(3, padded, nz), vmem(2, padded, nz), vmem(2, padded, nz), vmem(2, padded, nz), vmem(2, padded, nz),
        vmem(6, ext, nz), vmem(padded, nz), vmem(ext + nx, nz), vmem(ext, nz), vmem(2, ext, nz),
        vmem(STAGES, 2, 3, ny, nz), vmem(STAGES, 2, 3, ny, nz), vmem(2, 4, ny + 2, nz), vmem(2, 4, ny + 2, nz), vmem(2, 10, ny, nz), vmem(2, 10, ny, nz),
        line(5, cy + 2),
        line(), line(), line(group - 1), line(group - 1),
        line(), line(), line(n_group - 1), line(n_group - 1), line(),
        pltpu.SemaphoreType.REGULAR((8,)), pltpu.SemaphoreType.DMA((3 + ny,)),
        pltpu.SemaphoreType.DMA((STAGES, 4)), pltpu.SemaphoreType.DMA((STAGES, 4)),
        pltpu.SemaphoreType.DMA((6, 2)), pltpu.SemaphoreType.DMA((6, 2)),
        pltpu.SemaphoreType.DMA((4, kinds)), pltpu.SemaphoreType.DMA((4, kinds)),
    ]
    flat = lambda a: jnp.swapaxes(a, -3, -2).reshape(*a.shape[:-3], rows, nz)
    out = pl.pallas_call(
        functools.partial(kernel, (nx, ny, nz, n_gx, n_gy, group)),
        out_shape=jax.ShapeDtypeStruct((2, rows, nz), f32),
        in_specs=[pl.BlockSpec(memory_space=pl.ANY)] * 4,
        out_specs=pl.BlockSpec(memory_space=pl.ANY),
        scratch_shapes=scratch,
        compiler_params=pltpu.CompilerParams(collective_id=0, has_side_effects=True),
    )(flat(temps), flat(right_side), flat(exchange), flat(coupling))
    return jnp.swapaxes(out.reshape(2, ny, nx, nz), 1, 2)


def solution(mesh):
    return jax.shard_map(
        functools.partial(shards, mesh.shape["gx"], mesh.shape["gy"]),
        mesh=mesh,
        in_specs=(
            P(None, "gx", "gy", None),
            P(None, "gx", "gy", None),
            P("gx", "gy", None),
            P("gx", "gy", None),
        ),
        out_specs=P(None, "gx", "gy", None),
        check_vma=False,
    )
```

```python
import functools

import jax
import jax.numpy as jnp
from jax import lax
from jax.experimental import pallas as pl
from jax.experimental.pallas import tpu as pltpu
from jax.sharding import PartitionSpec as P

MESH = pl.DeviceIdType.MESH
EDGE = 8

solid_cap = 0.5
gas_cap = 0.02
flow_rate = 40.0
gas_conduct = 0.05
relaxation = 0.8
lump_factor = 0.25
STAGES = 4
REACH = 2


class Cells:
    def __init__(self, at, on, n, step=None, skip=None):
        self.at, self.on, self.n, self.step, self.skip = at, on, n, step, skip

    def coef(self, shift=0):
        return pl.ds(self.at + shift, self.n, stride=self.step)

    def field(self, shift=0):
        return pl.ds(self.on + shift, self.n, stride=self.skip)


def kernel(dims, temps, right, exch, coup, out, *scratch):
    nx, ny, nz, n_gx, n_gy, group = dims
    pitch = nx + EDGE
    cx, cy = nx // 2, ny // 2
    n_group = n_gy // group
    (e_in, c_f, f0, f1, f2, f3, f4, cf, fx, fy, diag, res, xs, xr, xs3, xr3, cs3, cr3, coarse,
     s_blk, o_blk, s_rec, o_rec, s_row, o_row, s_rrec, o_rrec, s_pre,
     news, in_sem, h_send, h_recv, w_send, w_recv, g_send, g_recv) = scratch
    P_, Q_, R_, FZ, B_S, B_G = range(6)
    CSUM, ISOL, CRES, SLOPE, OFFS = range(5)
    mine = slice(nx, (ny + 1) * nx)
    first_on = 2 * pitch
    ix, iy = lax.axis_index("gx"), lax.axis_index("gy")
    place, row = lax.rem(iy, group), lax.div(iy, group)

    loads = [
        pltpu.make_async_copy(temps.at[:, pl.ds(y * nx, nx)], f0.at[0:2, pl.ds((y + 2) * pitch, nx)], in_sem.at[3 + y])
        for y in range(ny)
    ]
    loads.append(pltpu.make_async_copy(exch, e_in.at[mine], in_sem.at[0]))
    more = [pltpu.make_async_copy(coup, c_f.at[mine], in_sem.at[1]), pltpu.make_async_copy(right, cf.at[B_S:B_G + 1, mine], in_sem.at[2])]
    for load in loads + more:
        load.start()

    barrier = pltpu.get_barrier_semaphore()

    def greet(gx, gy):
        pl.semaphore_signal(barrier, inc=1, device_id=(gx, gy), device_id_type=MESH)

    for d in range(1, group):
        greet(ix, row * group + lax.rem(place + d, group))
    near_rows = [(row + d < n_group, row + d) for d in range(1, min(REACH, n_group - 1) + 1)]
    near_rows += [(row >= d, row - d) for d in range(1, min(REACH, n_group - 1) + 1)]
    for there, other in near_rows:
        pl.when(there)(lambda other=other: greet(ix, other * group + place))
    up_y, down_y, up_x, down_x = iy < n_gy - 1, iy > 0, ix < n_gx - 1, ix > 0
    pl.when(up_y)(lambda: greet(ix, iy + 1))
    pl.when(down_y)(lambda: greet(ix, iy - 1))
    pl.when(up_x)(lambda: greet(ix + 1, iy))
    pl.when(down_x)(lambda: greet(ix - 1, iy))

    fields = (f0, f1, f2, f3, f4)
    plane_zero = jnp.zeros((nx, nz), jnp.float32)
    side_zero = jnp.zeros((ny, nz), jnp.float32)

    def clear_planes(y, far, face, line):
        for f in fields:
            for n in range(f.shape[0]):
                f[n, (y + 2) * pitch:(y + 2) * pitch + nx, :] = plane_zero
        for n in range(2):
            f2[n, (far + 2) * pitch:(far + 2) * pitch + nx, :] = plane_zero
        for n in range(6):
            cf[n, (y + 1) * nx:(y + 2) * nx, :] = plane_zero
        fx[(y + 2) * pitch - 8:(y + 2) * pitch + nx, :] = jnp.zeros((nx + 8, nz), jnp.float32)
        fy[face * nx:(face + 1) * nx, :] = plane_zero
        for n in range(5):
            coarse[n, line] = jnp.zeros((cx, nz), jnp.float32)

    def clear_sides(side):
        for st in range(STAGES):
            for n in range(3 if st == 0 else 2):
                xr[st, side, n] = side_zero
        for n in range(4):
            xr3[side, n] = jnp.zeros((ny + 2, nz), jnp.float32)
        for n in range(10):
            cr3[side, n] = side_zero

    pl.when(jnp.logical_not(down_y))(lambda: clear_planes(-1, -2, 0, 0))
    pl.when(jnp.logical_not(up_y))(lambda: clear_planes(ny, ny + 1, ny + 2, cy + 1))
    pl.when(jnp.logical_not(down_x))(lambda: clear_sides(0))
    pl.when(jnp.logical_not(up_x))(lambda: clear_sides(1))
    for d in range(1, n_group):

        @pl.when(row < d)
        def _():
            s_rrec[d - 1] = jnp.ones((cx, nz), jnp.float32)
            o_rrec[d - 1] = jnp.zeros((cx, nz), jnp.float32)

    def remote(src, dst, send, recv, to):
        return pltpu.make_async_remote_copy(
            src_ref=src, dst_ref=dst, send_sem=send, recv_sem=recv, device_id=to, device_id_type=MESH)

    def halo_copies(st):
        f = fields[st]
        nf = f.shape[0]
        plane = lambda y: f.at[:, (y + 2) * pitch:(y + 2) * pitch + nx]
        sides = (xs3, xr3) if st == 3 else (xs.at[st, :, :nf], xr.at[st, :, :nf])
        parts = [
            (up_x, down_x, sides[0].at[1], sides[1].at[0], (ix + 1, iy)),
            (down_x, up_x, sides[0].at[0], sides[1].at[1], (ix - 1, iy)),
        ]
        if st < 3:
            parts += [
                (up_y, down_y, plane(ny - 1), plane(-1), (ix, iy + 1)),
                (down_y, up_y, plane(0), plane(ny), (ix, iy - 1)),
            ]
        return [
            (sends, receives, remote(src, dst, h_send.at[st, i], h_recv.at[st, i], to))
            for i, (sends, receives, src, dst, to) in enumerate(parts)
        ]

    def side_rows(st, x):
        more = 1 if st == 3 else 0
        return pl.ds(first_on - more * pitch + x, ny + 2 * more, stride=pitch)

    def send_halo(st):
        f = fields[st]
        for n in range(f.shape[0]):
            for side, x, deeper in ((0, 0, 1), (1, nx - 1, nx - 2)):
                if st == 3:
                    xs3[side, n] = f[n, side_rows(st, x), :]
                    xs3[side, 2 + n] = f[n, side_rows(st, deeper), :]
                else:
                    xs[st, side, n] = f[n, side_rows(st, x), :]
        copies = halo_copies(st)
        for sends, _, copy in copies[2:] + copies[:2]:
            pl.when(sends)(copy.start)

    def take_halo(st):
        f = fields[st]
        for sends, receives, copy in halo_copies(st):
            pl.when(sends)(copy.wait_send)
            pl.when(receives)(copy.wait_recv)
        for n in range(f.shape[0]):
            for side, x, deeper in ((0, -1, -2), (1, nx, nx + 1)):
                if st == 3:
                    f[n, side_rows(st, x), :] = xr3[side, n]
                    f[n, side_rows(st, deeper), :] = xr3[side, 2 + n]
                else:
                    f[n, side_rows(st, x), :] = xr[st, side, n]

    def deep_copies(kind):
        if kind == 5:
            return [
                (up_x, down_x, remote(cs3.at[1], cr3.at[0], w_send.at[5, 0], w_recv.at[5, 0], (ix + 1, iy))),
                (down_x, up_x, remote(cs3.at[0], cr3.at[1], w_send.at[5, 1], w_recv.at[5, 1], (ix - 1, iy))),
            ]
        near = lambda ref, low, high: (ref.at[low:high] if len(ref.shape) == 2 else ref.at[:, low:high])
        if kind == 0:
            ups, downs = (cf, ny * nx, 0, nx), (cf, nx, (ny + 1) * nx, nx)
        elif kind == 1:
            ups = (fx, (ny + 1) * pitch - 8, pitch - 8, nx + 8)
            downs = (fx, 2 * pitch - 8, (ny + 2) * pitch - 8, nx + 8)
        elif kind == 2:
            ups, downs = (fy, ny * nx, 0, nx), (fy, 2 * nx, (ny + 2) * nx, nx)
        elif kind == 3:
            ups, downs = (f2, ny * pitch, 0, nx), (f2, 3 * pitch, (ny + 3) * pitch, nx)
        else:
            ups, downs = (coarse, cy, 0, 1), (coarse, 1, cy + 1, 1)
        return [
            (sends, receives, remote(near(ref, src, src + n), near(ref, dst, dst + n),
                                     w_send.at[kind, i], w_recv.at[kind, i], to))
            for i, (sends, receives, to, (ref, src, dst, n)) in enumerate((
                (up_y, down_y, (ix, iy + 1), ups), (down_y, up_y, (ix, iy - 1), downs)))
        ]

    def send_deep(*kinds):
        for kind in kinds:
            for sends, _, copy in deep_copies(kind):
                pl.when(sends)(copy.start)

    def take_deep(*kinds):
        for kind in kinds:
            for sends, receives, copy in deep_copies(kind):
                pl.when(sends)(copy.wait_send)
                pl.when(receives)(copy.wait_recv)

    def group_copies(kind, block, received):
        return [
            remote(block, received.at[d - 1], g_send.at[kind, d - 1], g_recv.at[kind, d - 1],
                   (ix, row * group + lax.rem(place + d, group)))
            for d in range(1, group)
        ]

    def row_copies(kind, block, received):
        return [
            (row + d < n_group, row >= d, remote(
                block, received.at[d - 1], g_send.at[kind, d - 1], g_recv.at[kind, d - 1],
                (ix, (row + d) * group + place)))
            for d in range(1, n_group)
        ]

    def plane(y):
        return Cells((y + 1) * nx, (y + 2) * pitch, nx)

    def inner(body, low=1, high=ny - 1, unroll=2):
        def step(y, _):
            body(Cells(pl.multiple_of((y + 1) * nx, 8), pl.multiple_of((y + 2) * pitch, 8), nx))
            return 0

        lax.fori_loop(low, high, step, 0, unroll=unroll)

    def columns(body, more=0, at=(0, nx - 1)):
        for x in at:
            body(Cells((1 - more) * nx + x, (2 - more) * pitch + x, ny + 2 * more, nx, pitch))

    def outer(body):
        body(plane(0))
        body(plane(ny - 1))
        columns(body)

    def conductivity(u):
        t = f0[0, u.field(), :]
        f0[2, u.field(), :] = 1.0 + 4.0 * e_in[u.coef(), :] * (t * t * t)

    for load in loads:
        load.wait()
    inner(conductivity, 0, ny)
    n_some = sum(v.astype(jnp.int32) for v in (up_y, down_y, up_x, down_x, *(there for there, _ in near_rows)))
    pl.semaphore_wait(barrier, group - 1 + n_some)
    send_halo(0)

    rounds = max(0, -(-(n_group - 1 - REACH) // REACH))

    def tell(k):
        if k < rounds:

            @pl.when(row >= REACH)
            def _():
                pl.semaphore_signal(
                    news.at[k], inc=1, device_id=(ix, (row - REACH) * group + place), device_id_type=MESH)

    def hear(k):
        if k < rounds:
            pl.when(row + REACH < n_group)(lambda: pl.semaphore_wait(news.at[k], 1))

    tell(0)
    for load in more:
        load.wait()

    def block_sum(load, j, step):
        total = None
        for a in (0, step):
            for b in (0, 1):
                part = load(2 * j * step + a + b)
                total = part if total is None else total + part
        return total

    s_all = None
    for j in range(cy):
        cs = block_sum(lambda at: c_f[pl.ds(nx + at, cx, stride=2), :], j, nx)
        cond = block_sum(lambda at: f0[2, pl.ds(first_on + at, cx, stride=2), :], j, pitch)
        inv_solid = 1.0 / (4.0 * solid_cap + cs + lump_factor * cond)
        inv_denom = 1.0 / (4.0 * gas_cap + cs + 2.0 * flow_rate - cs * cs * inv_solid)
        slope = 2.0 * flow_rate * inv_denom
        coarse[CSUM, j + 1], coarse[ISOL, j + 1], coarse[SLOPE, j + 1] = cs, inv_solid, slope
        s_all = slope if s_all is None else s_all * slope
    s_blk[...] = s_all
    for copy in group_copies(0, s_blk, s_rec):
        copy.start()

    lane = lax.broadcasted_iota(jnp.int32, (1, nz), 1)
    not_last = (lane < nz - 1).astype(jnp.float32)
    not_first = (lane > 0).astype(jnp.float32)
    gas_zp = gas_conduct * 0.25 * not_last
    gas_zm = gas_conduct * 0.25 * not_first

    def set_up(u):
        c = f0[2, u.field(), :]
        xp = 0.5 * (c + f0[2, u.field(1), :])
        xm = 0.5 * (c + f0[2, u.field(-1), :])
        yp = 0.5 * (c + f0[2, u.field(pitch), :])
        ym = 0.5 * (c + f0[2, u.field(-pitch), :])
        zp = 0.125 * (c + not_last * pltpu.roll(c, nz - 1, 1))
        zm = 0.125 * (c + not_first * pltpu.roll(c, 1, 1))
        fx[u.field(), :] = xp
        if u.step is None:
            fx[pl.ds(u.on - 8, 8), :] = 0.5 * (f0[2, pl.ds(u.on - 8, 8), :] + f0[2, pl.ds(u.on - 7, 8), :])
        else:
            fx[u.field(-1), :] = xm
        fy[u.coef(), :] = ym
        fy[u.coef(nx), :] = yp
        cf[FZ, u.coef(), :] = not_last * zp
        k = c_f[u.coef(), :]
        sd = solid_cap + k + (((xp + xm) + (yp + ym)) + (zp + zm))
        gd = (gas_cap + flow_rate + gas_conduct * 2.0 * 2.25) + k
        w = relaxation / (sd * gd - k * k)
        diag[u.coef(), :] = sd
        cf[P_, u.coef(), :] = gd * w
        cf[Q_, u.coef(), :] = k * w
        cf[R_, u.coef(), :] = sd * w

    class Given:
        def __init__(self, x, side):
            self.on, self.side = first_on + x, side

        def field(self, shift=0):
            return pl.ds(self.on + shift, ny, stride=pitch)

        def own(self, n):
            return cr3[self.side, n]

        def faces(self):
            return tuple(cr3[self.side, n] for n in (6, 7, 8, 9))

    def own(u, n):
        return u.own(n) if isinstance(u, Given) else cf[n, u.coef(), :]

    def faces(u):
        if isinstance(u, Given):
            return u.faces()
        return fx[u.field(-1), :], fx[u.field(), :], fy[u.coef(), :], fy[u.coef(nx), :]

    def beside(f, u):
        s = f[0, u.field(), :]
        g = f[1, u.field(), :]
        z = own(u, FZ)
        xm, xp, ym, yp = faces(u)
        hs = own(u, B_S)
        hs += yp * f[0, u.field(pitch), :]
        hs += ym * f[0, u.field(-pitch), :]
        hs += xp * f[0, u.field(1), :]
        hs += xm * f[0, u.field(-1), :]
        hs += z * pltpu.roll(s, nz - 1, 1) + pltpu.roll(z * s, 1, 1)
        hg = own(u, B_G)
        hg += (flow_rate + gas_conduct) * f[1, u.field(-pitch), :]
        hg += gas_conduct * (f[1, u.field(pitch), :] + (f[1, u.field(-1), :] + f[1, u.field(1), :]))
        hg += gas_zp * pltpu.roll(g, nz - 1, 1) + gas_zm * pltpu.roll(g, 1, 1)
        return s, g, hs, hg

    def relaxed(f, u):
        s, g, hs, hg = beside(f, u)
        p, q, r = own(u, P_), own(u, Q_), own(u, R_)
        keep = 1.0 - relaxation
        return keep * s + (p * hs + q * hg), keep * g + (q * hs + r * hg)

    def sweep(f, new):
        def body(u):
            new[0, u.field(), :], new[1, u.field(), :] = relaxed(f, u)

        return body

    inner(set_up)
    inner(sweep(f0, f1))
    hear(0)
    tell(1)
    take_halo(0)
    outer(set_up)
    outer(sweep(f0, f1))
    send_halo(1)
    for side, x in ((0, 0), (1, nx - 1)):
        u = Cells(nx + x, first_on + x, ny, nx, pitch)
        for n in range(6):
            cs3[side, n] = cf[n, u.coef(), :]
        cs3[side, 6], cs3[side, 7] = fx[u.field(-1), :], fx[u.field(), :]
        cs3[side, 8], cs3[side, 9] = fy[u.coef(), :], fy[u.coef(nx), :]
    send_deep(0, 1, 2, 5)
    inner(sweep(f1, f2))

    def upstream(d):
        return jnp.full((cx, nz), place, jnp.int32) >= d

    for copy in group_copies(0, s_blk, s_rec):
        copy.wait()
    s_before = s_after = jnp.ones((cx, nz), jnp.float32)
    for d in range(1, group):
        s_d = s_rec[d - 1]
        s_before = jnp.where(upstream(d), s_before * s_d, s_before)
        s_after = jnp.where(upstream(d), s_after, s_after * s_d)
    s_pre[...] = s_before
    s_row[...] = s_before * s_blk[...] * s_after
    hear(1)
    tell(2)

    take_halo(1)
    outer(sweep(f1, f2))
    send_halo(2)
    send_deep(3)

    def residual(u):
        s, g, hs, hg = beside(f2, u)
        k = c_f[u.coef(), :]
        gd = (gas_cap + flow_rate + gas_conduct * 2.0 * 2.25) + k
        res[0, u.coef(), :] = hs - (diag[u.coef(), :] * s - k * g)
        res[1, u.coef(), :] = hg - (gd * g - k * s)

    inner(residual)
    for k in range(2, rounds):
        hear(k)
        tell(k + 1)
    for sends, _, copy in row_copies(1, s_row, s_rrec):
        pl.when(sends)(copy.start)
    take_halo(2)
    outer(residual)

    state = jnp.zeros((cx, nz), jnp.float32)
    for j in range(cy):
        r_s = block_sum(lambda at: res[0, pl.ds(nx + at, cx, stride=2), :], j, nx)
        r_g = block_sum(lambda at: res[1, pl.ds(nx + at, cx, stride=2), :], j, nx)
        slope = coarse[SLOPE, j + 1]
        offset = (r_g + coarse[CSUM, j + 1] * r_s * coarse[ISOL, j + 1]) * (slope * (0.5 / flow_rate))
        coarse[CRES, j + 1], coarse[OFFS, j + 1] = r_s, offset
        state = slope * state + offset
    o_blk[...] = state
    for copy in group_copies(2, o_blk, o_rec):
        copy.start()
    send_deep(4)
    for sends, receives, copy in row_copies(1, s_row, s_rrec):
        pl.when(sends)(copy.wait_send)
        pl.when(receives)(copy.wait_recv)
    for copy in group_copies(2, o_blk, o_rec):
        copy.wait()
    state = jnp.zeros((cx, nz), jnp.float32)
    for d in range(group - 1, 0, -1):
        state = jnp.where(upstream(d), s_rec[d - 1] * state + o_rec[d - 1], state)
    before = state
    state = s_blk[...] * state + o_blk[...]
    for d in range(group - 1, 0, -1):
        state = jnp.where(upstream(d), state, s_rec[d - 1] * state + o_rec[d - 1])
    o_row[...] = state
    for sends, _, copy in row_copies(3, o_row, o_rrec):
        pl.when(sends)(copy.start)
    for sends, receives, copy in row_copies(3, o_row, o_rrec):
        pl.when(sends)(copy.wait_send)
        pl.when(receives)(copy.wait_recv)
    state = jnp.zeros((cx, nz), jnp.float32)
    for d in range(n_group - 1, 0, -1):
        state = s_rrec[d - 1] * state + o_rrec[d - 1]
    error = s_pre[...] * state + before
    take_deep(0, 1, 2, 3, 4, 5)
    for j in range(-1, cy + 1):
        if j >= 0:
            error = coarse[SLOPE, j + 1] * error + coarse[OFFS, j + 1]
        solid_error = (coarse[CRES, j + 1] + coarse[CSUM, j + 1] * error) * coarse[ISOL, j + 1]
        for y in (2 * j, 2 * j + 1):
            for b in (0, 1):
                at = pl.ds((y + 2) * pitch + b, cx, stride=2)
                f3[0, at, :] = f2[0, at, :] + solid_error
                f3[1, at, :] = f2[1, at, :] + error

    def last(u):
        out[0, u.coef(-nx), :], out[1, u.coef(-nx), :] = relaxed(f4, u)

    send_halo(3)
    inner(sweep(f3, f4), -1, ny + 1)
    inner(last, 0, ny)
    take_halo(3)
    columns(sweep(f3, f4), 1)
    sweep(f3, f4)(Given(-1, 0))
    sweep(f3, f4)(Given(nx, 1))
    columns(last, 0, (0, 1, nx - 2, nx - 1))


def shards(n_gx, n_gy, temps, right_side, exchange, coupling):
    _, nx, ny, nz = temps.shape
    group = 8 if n_gy % 8 == 0 else 2
    n_group = n_gy // group
    rows, cx, cy = nx * ny, nx // 2, ny // 2
    f32 = jnp.float32
    padded = (nx + EDGE) * (ny + 4)
    ext = rows + 2 * nx
    kinds = max(group, n_group) - 1
    vmem = lambda *shape: pltpu.VMEM(shape, f32)
    line = lambda *lead: pltpu.VMEM((*lead, cx, nz), f32)
    scratch = [
        vmem(ext, nz), vmem(ext, nz),
        vmem(3, padded, nz), vmem(2, padded, nz), vmem(2, padded, nz), vmem(2, padded, nz), vmem(2, padded, nz),
        vmem(6, ext, nz), vmem(padded, nz), vmem(ext + nx, nz), vmem(ext, nz), vmem(2, ext, nz),
        vmem(STAGES, 2, 3, ny, nz), vmem(STAGES, 2, 3, ny, nz), vmem(2, 4, ny + 2, nz), vmem(2, 4, ny + 2, nz), vmem(2, 10, ny, nz), vmem(2, 10, ny, nz),
        line(5, cy + 2),
        line(), line(), line(group - 1), line(group - 1),
        line(), line(), line(n_group - 1), line(n_group - 1), line(),
        pltpu.SemaphoreType.REGULAR((8,)), pltpu.SemaphoreType.DMA((3 + ny,)),
        pltpu.SemaphoreType.DMA((STAGES, 4)), pltpu.SemaphoreType.DMA((STAGES, 4)),
        pltpu.SemaphoreType.DMA((6, 2)), pltpu.SemaphoreType.DMA((6, 2)),
        pltpu.SemaphoreType.DMA((4, kinds)), pltpu.SemaphoreType.DMA((4, kinds)),
    ]
    flat = lambda a: jnp.swapaxes(a, -3, -2).reshape(*a.shape[:-3], rows, nz)
    out = pl.pallas_call(
        functools.partial(kernel, (nx, ny, nz, n_gx, n_gy, group)),
        out_shape=pltpu.VMEM((2, rows, nz), f32),
        in_specs=[pl.BlockSpec(memory_space=pl.ANY)] * 4,
        out_specs=pl.BlockSpec(memory_space=pltpu.VMEM),
        scratch_shapes=scratch,
        compiler_params=pltpu.CompilerParams(collective_id=0, has_side_effects=True),
    )(flat(temps), flat(right_side), flat(exchange), flat(coupling))
    return jnp.swapaxes(out.reshape(2, ny, nx, nz), 1, 2)


def solution(mesh):
    return jax.shard_map(
        functools.partial(shards, mesh.shape["gx"], mesh.shape["gy"]),
        mesh=mesh,
        in_specs=(
            P(None, "gx", "gy", None),
            P(None, "gx", "gy", None),
            P("gx", "gy", None),
            P("gx", "gy", None),
        ),
        out_specs=P(None, "gx", "gy", None),
        check_vma=False,
    )
```
